32 devices in a mesh: dom: 8 (over z, x), grp: 4 (over y, core).
Axes of the slice: x: 2, y: 2, z: 4, core: 2. Of those that a mesh axis runs over, the one named last changes fastest.
Arguments:
- features: bfloat16 [32768, 512], P(('dom', 'grp')), may hold values from -6 to 6
- tile_src: int32 [256, 8], P(('dom', 'grp')), may hold values from 0 to 8
- tile_val: bfloat16 [256, 8, 128, 128], P(('dom', 'grp')), may hold values from -0.1875 to 0.1875
- send_sel: int32 [32, 8], P(('dom', 'grp')), may hold values from 0 to 63
- stale_features: bfloat16 [4096, 512], P(('dom', 'grp')), may hold values from -5 to 5
- stale_grads: bfloat16 [4096, 512], P(('dom', 'grp')), may hold values from -6 to 6
- out_grad: bfloat16 [32768, 512], P(('dom', 'grp')), may hold values from -6 to 6
- master: float32 [2, 512, 512], P(None, ('dom', 'grp')), may hold values from -0.25 to 0.25
- moment_first: float32 [2, 512, 512], P(None, ('dom', 'grp')), may hold values from -0.0234375 to 0.0234375
- moment_second: float32 [2, 512, 512], P(None, ('dom', 'grp')), may hold values from 6.1035155e-07 to 1.5258789e-05
Outputs:
- layer_out: bfloat16 [32768, 512], P(('dom', 'grp'))
- fresh_features: bfloat16 [4096, 512], P(('dom', 'grp'))
- fresh_grads: bfloat16 [4096, 512], P(('dom', 'grp'))
- master_next: float32 [2, 512, 512], P(None, ('dom', 'grp'))
- weights_next: bfloat16 [2, 512, 512], replicated
The draws below stay inside these ranges and needn't reach their ends.
Inputs may be any that keep to these rules, and one draw needn't show every extreme that they name: `tile_src`: A value below 8 names a local row block; 8 + b names boundary block b.
All inputs are finite; a program needn't handle non-finite values.
Results may differ from the reference program's by a relative error of at most 0.005.
The reference program's roundings to bfloat16 on the way count: a program that leaves them out, or rounds other values in their place, can miss the bound.
Values may be sent and summed in bfloat16 or wider, within the bound.
No kernel may reach another device: no remote copies, remote signals or barrier semaphores. Data moves between devices by JAX's collectives and lax.ppermute only.
A program may use at most 128 MiB of HBM per device.

```python
import math
import jax
import jax.numpy as jnp
from jax import lax

F = 512
BLOCK = 128
TILES = 8
PIECE = 16
STEP = 10
RB = 8
NODES_DEV = 1024
TOTAL_NODES = 32768
ALL_BLOCKS = 256
ALL_RIM = 4096
N_DOM = 8
N_GRP = 4


def with_ends(drawn, stream_key, low, high):
    index_at = [jax.random.randint(jax.random.fold_in(stream_key, axis), (), 0, length) for axis, length in enumerate(drawn.shape)]
    longest = drawn.shape.index(max(drawn.shape))
    beside = index_at[:longest] + [(index_at[longest] + 1) % drawn.shape[longest]] + index_at[longest + 1:]
    return drawn.at[tuple(index_at)].set(low).at[tuple(beside)].set(high)


def level_of(key, extent, split, smallest, top_value):
    gain = 1.0
    for axis_at, blocks in split:
        steps = jax.random.uniform(jax.random.fold_in(jax.random.fold_in(key, 6), axis_at), (blocks,), jnp.float32, smallest / len(split), top_value / len(split))
        gain = gain * jnp.repeat(jnp.exp(steps), extent[axis_at] // blocks).reshape((-1,) + (1,) * (len(extent) - 1 - axis_at))
    return gain


def gaussian(key, extent, scale, bound, cuts=(), kind=jnp.bfloat16):
    factor_of = level_of(key, extent, cuts, -0.22, 0.18) if cuts else 1.0
    array = jax.random.normal(key, extent, jnp.float32) * scale * factor_of
    return jnp.minimum(jnp.maximum(array, -bound), bound).astype(kind)


def setup_inputs(seed: int = 0) -> dict:
    key_list = jax.random.split(jax.random.key(seed), 11)
    features = gaussian(key_list[0], (TOTAL_NODES, F), 1.0, 6.0, ((0, 32),))
    tile_src = with_ends(jax.random.randint(key_list[1], (ALL_BLOCKS, TILES), 0, RB + N_DOM * PIECE // BLOCK), jax.random.fold_in(key_list[1], 1), 0, (RB + N_DOM * PIECE // BLOCK) - 1).astype(jnp.int32)
    tile_val = gaussian(key_list[2], (ALL_BLOCKS, TILES, BLOCK, BLOCK), (TILES * BLOCK) ** -0.5, 0.1875, ((0, 32),))
    send_sel = with_ends(jax.random.randint(key_list[3], (N_DOM * N_GRP, N_DOM), 0, NODES_DEV // PIECE), jax.random.fold_in(key_list[3], 1), 0, (NODES_DEV // PIECE) - 1).astype(jnp.int32)
    stale_features = gaussian(key_list[4], (ALL_RIM, F), 0.7, 5.0, ((0, 32),))
    stale_grads = gaussian(key_list[5], (ALL_RIM, F), 1.0, 6.0, ((0, 32),))
    out_grad = gaussian(key_list[6], (TOTAL_NODES, F), 1.0, 6.0, ((0, 32),))
    master = gaussian(key_list[7], (2, F, F), F ** -0.5, 0.25, ((1, 32),), jnp.float32)
    moment_first = gaussian(key_list[8], (2, F, F), (0.3 / TOTAL_NODES ** 0.5), 0.0234375, ((1, 32),), jnp.float32)
    moment_second = jnp.clip(jnp.exp(math.log(1.52587890625e-05) - 3.218876 * jax.random.uniform(key_list[9], (2, F, F), jnp.float32) ** level_of(key_list[9], (2, F, F), ((1, 32),), -0.2, 0.2)), 6.103515488575795e-07, 1.52587890625e-05)
    return dict(features=features, tile_src=tile_src, tile_val=tile_val, send_sel=send_sel, stale_features=stale_features, stale_grads=stale_grads, out_grad=out_grad, master=master, moment_first=moment_first, moment_second=moment_second)


decay_first = 0.9
decay_second = 0.95
learn_rate = 0.01
epsilon = 1e-08

def aggregate(local_rows, rim_rows, tile_block, sources):
    lookup = jnp.concatenate([local_rows, rim_rows], 0).reshape(-1, BLOCK, F)
    picked = lookup[sources]
    total = jnp.einsum('rtij,rtjf->rif', tile_block.astype(jnp.float32), picked.astype(jnp.float32))
    return total.reshape(-1, F)

def spread(tile_block, sources, upstream):
    contrib = jnp.einsum('rtij,rif->rtjf', tile_block.astype(jnp.float32), upstream.reshape(RB, BLOCK, F).astype(jnp.float32))
    slots = RB + N_DOM * PIECE // BLOCK
    onehot = (sources.reshape(-1)[:, None] == jnp.arange(slots, dtype=jnp.int32)[None, :]).astype(jnp.float32)
    total = jnp.einsum('kb,kjf->bjf', onehot, contrib.reshape(RB * TILES, BLOCK, F), precision=lax.Precision.HIGHEST)
    return total.reshape(-1, F)

def swap_peers(pieces):
    return pieces.reshape(N_DOM, N_GRP, N_DOM, PIECE, F).transpose(2, 1, 0, 3, 4).reshape(-1, F)

def reference(features, tile_src, tile_val, send_sel, stale_features, stale_grads, out_grad, master, moment_first, moment_second):
    devices = N_DOM * N_GRP
    weights = master.astype(jnp.bfloat16)
    selects = send_sel.reshape(devices, N_DOM)
    tile_blocks = tile_val.reshape(devices, RB, TILES, BLOCK, BLOCK)
    source_ids = tile_src.reshape(devices, RB, TILES)

    def outgoing(node_rows):
        pieces = node_rows.reshape(devices, -1, PIECE, F)
        chosen = jax.vmap(lambda group, picks: group[picks])(pieces, selects)
        return swap_peers(chosen.reshape(-1, F))

    def aggregate_all(node_rows, rim_all):
        packs = (node_rows.reshape(devices, RB * BLOCK, F), rim_all.reshape(devices, N_DOM * PIECE, F), tile_blocks, source_ids)
        return lax.map(lambda packed: aggregate(packed[0], packed[1], packed[2], packed[3]), packs).reshape(-1, F)
    p_first = aggregate_all(features, outgoing(features)).astype(jnp.bfloat16)
    z_first = jnp.dot(p_first, weights[0], preferred_element_type=jnp.float32)
    h_first = jax.nn.silu(z_first).astype(jnp.bfloat16)
    fresh_features = outgoing(h_first)
    p_second = aggregate_all(h_first, stale_features).astype(jnp.bfloat16)
    layer_out = jnp.dot(p_second, weights[1], preferred_element_type=jnp.float32).astype(jnp.bfloat16)
    upstream = jnp.dot(out_grad, weights[1].T, preferred_element_type=jnp.float32).astype(jnp.bfloat16)
    g_second = jnp.dot(p_second.T, out_grad, preferred_element_type=jnp.float32) / TOTAL_NODES
    packs = (tile_blocks, source_ids, upstream.reshape(devices, RB * BLOCK, F))
    spreads = lax.map(lambda packed: spread(packed[0], packed[1], packed[2]), packs)
    local_part = spreads[:, :RB * BLOCK]
    fresh_grads = swap_peers(spreads[:, RB * BLOCK:].astype(jnp.bfloat16).reshape(-1, F))
    piece_count = RB * BLOCK // PIECE
    placing = (selects[:, :, None] == jnp.arange(piece_count, dtype=jnp.int32)[None, None, :]).astype(jnp.float32)
    stale_slots = stale_grads.reshape(devices, N_DOM, PIECE, F).astype(jnp.float32)
    placed = jnp.einsum('dpq,dprf->dqrf', placing, stale_slots, precision=lax.Precision.HIGHEST)
    d_first = (local_part + placed.reshape(devices, -1, F)).reshape(-1, F)
    sigma = jax.nn.sigmoid(z_first)
    dz = (d_first * sigma * (1.0 + z_first * (1.0 - sigma))).astype(jnp.bfloat16)
    g_first = jnp.dot(p_first.T, dz, preferred_element_type=jnp.float32) / TOTAL_NODES
    grads = jnp.stack([g_first, g_second])
    moment_new = decay_first * moment_first + (1.0 - decay_first) * grads
    second_new = decay_second * moment_second + (1.0 - decay_second) * grads * grads
    update = moment_new / (1.0 - decay_first ** STEP) / (jnp.sqrt(second_new / (1.0 - decay_second ** STEP)) + epsilon)
    master_next = master - learn_rate * update
    weights_next = master_next.astype(jnp.bfloat16)
    return (layer_out, fresh_features, fresh_grads, master_next, weights_next)
```

```python
import functools

import jax
import jax.numpy as jnp
import numpy as np
from jax import lax
from jax.experimental import pallas as pl
from jax.experimental.pallas import tpu as pltpu
from jax.sharding import PartitionSpec as P

STEP = 10


decay_first = 0.9
decay_second = 0.95
learn_rate = 0.01
epsilon = 1e-08

F32 = jnp.float32
BF16 = jnp.bfloat16
AXES = ("dom", "grp")
VMEM = pl.BlockSpec(memory_space=pltpu.VMEM)
SMEM = pl.BlockSpec(memory_space=pltpu.SMEM)
ANY = pl.BlockSpec(memory_space=pl.ANY)
PACK = 16


def plan_stages(nd, ng):
    dom_bits = [1 << i for i in range(nd.bit_length() - 1)]
    grp_bits = [1 << i for i in range(ng.bit_length() - 1)]
    groups = [[(0, b) for b in grp_bits[:1]], [(a, 0) for a in dom_bits[:1]] + [(0, b) for b in grp_bits[1:2]]]
    rest = [(a, 0) for a in dom_bits[1:]] + [(0, b) for b in grp_bits[2:]]
    groups += [rest[i : i + 2] for i in range(0, len(rest), 2)]
    stages = []
    for bits in groups:
        members = [(0, 0)]
        for a, b in bits:
            members = members + [(a ^ x, b ^ y) for x, y in members]
        if len(members) > 1:
            stages.append(members)
    return stages


def relative_order(stages):
    order = [(0, 0)]
    for members in stages:
        order = [(a ^ x, b ^ y) for a, b in order for x, y in members]
    return order


def swap(x, mask):
    nd, ng = lax.axis_size("dom"), lax.axis_size("grp")
    pairs = [(k, ((k // ng) ^ mask[0]) * ng + ((k % ng) ^ mask[1])) for k in range(nd * ng)]
    return lax.ppermute(x, AXES, pairs)


def gather_relative(shard, stages):
    held = shard
    for members in stages[:0:-1]:
        held = jnp.concatenate([held] + [swap(held, m) for m in members[1:]], 0)
    return held, swap(held, stages[0][1])


def reduce_relative(keep, send, stages):
    got = swap(send, stages[0][1])
    total = keep.astype(F32) + got.astype(F32)
    for members in stages[1:]:
        pieces = jnp.split(total.astype(BF16), len(members), 0)
        got = [swap(p, m) for p, m in zip(pieces[1:], members[1:])]
        total = pieces[0].astype(F32)
        for g in got:
            total = total + g.astype(F32)
    return total


def dot(a, b, ca=1, cb=0):
    return lax.dot_general(a, b, (((ca,), (cb,)), ((), ())), preferred_element_type=F32)


def rows(start, size):
    return pl.ds(pl.multiple_of(start * size, size), size)


def pick_kernel(piece, count, sel_ref, rows_ref, out_ref, sems):
    copies = []
    for p in range(count):
        copies.append(
            pltpu.make_async_copy(
                rows_ref.at[rows(sel_ref[p], piece), :], out_ref.at[pl.ds(p * piece, piece), :], sems.at[p]
            )
        )
    for c in copies:
        c.start()
    for c in copies:
        c.wait()


def aggregate_block(i, src_ref, tile_ref, table_ref):
    tiles, edge = tile_ref.shape[1], tile_ref.shape[2]
    left = jnp.concatenate([tile_ref[i, t] for t in range(tiles)], 1)
    right = jnp.concatenate([table_ref[rows(src_ref[i, t], edge), :] for t in range(tiles)], 0)
    return dot(left, right).astype(BF16)


def fill_table(table_ref, local_ref, rim_ref):
    local = local_ref.shape[0]
    table_ref[:local, :] = local_ref[...]
    table_ref[local:, :] = rim_ref[...]


def first_kernel(src_ref, feat_ref, rim_ref, tile_ref, out_ref, table_ref):
    blocks, edge = tile_ref.shape[0], tile_ref.shape[2]
    fill_table(table_ref, feat_ref, rim_ref)

    def body(i, carry):
        out_ref[rows(i, edge), :] = aggregate_block(i, src_ref, tile_ref, table_ref)
        return carry

    lax.fori_loop(0, blocks, body, 0)


def assemble(dst_ref, tab_ref, parts):
    count = tab_ref.shape[0]
    size = dst_ref.shape[0] // count
    half = count // len(parts)
    for r in range(count):
        src = parts[r // half]
        at = (r % half) * size
        dst_ref[rows(tab_ref[r], size), :] = src[at : at + size, :]


def scatter_grad(tab_ref, full_ref, outs):
    count = tab_ref.shape[0]
    size = full_ref.shape[0] // count
    half = count // len(outs)
    for r in range(count):
        at = (r % half) * size
        outs[r // half][at : at + size, :] = full_ref[rows(tab_ref[r], size), :].astype(BF16)


def weight_grad(full_ref, left_ref, right_ref):
    step = 128
    for m in range(full_ref.shape[0] // step):
        cols = slice(m * step, (m + 1) * step)
        full_ref[cols, :] = dot(left_ref[:, cols], right_ref[...], 0, 0)


def spread_kernel(src_ref, sel_ref, tab_ref, og_ref, tile_ref, lo_ref, hi_ref, stale_ref, acc_ref, w_ref):
    blocks, tiles, edge = tile_ref.shape[0], tile_ref.shape[1], tile_ref.shape[2]
    peers = sel_ref.shape[0]
    piece = stale_ref.shape[0] // peers
    assemble(w_ref, tab_ref, (lo_ref, hi_ref))
    acc_ref[...] = jnp.zeros_like(acc_ref)

    def body(i, carry):
        up = dot(og_ref[rows(i, edge), :], w_ref[...], 1, 1).astype(BF16)
        for t in range(tiles):
            at = rows(src_ref[i, t], edge)
            acc_ref[at, :] += dot(tile_ref[i, t], up, 0, 0)
        return carry

    lax.fori_loop(0, blocks, body, 0)

    def place(p, carry):
        at = rows(sel_ref[p], piece)
        acc_ref[at, :] += stale_ref[rows(p, piece), :].astype(F32)
        return carry

    lax.fori_loop(0, peers, place, 0)


def hidden_kernel(
    sel_ref, tab_ref, p_ref, acc_ref, lo_ref, hi_ref, h_ref, route_ref, keep_ref, send_ref, w_ref, dz_ref, full_ref
):
    step = 128
    local = p_ref.shape[0]
    peers = sel_ref.shape[0]
    piece = (acc_ref.shape[0] - local) // peers
    assemble(w_ref, tab_ref, (lo_ref, hi_ref))

    def body(i, carry):
        at = rows(i, step)
        z = dot(p_ref[at, :], w_ref[...])
        s = 1.0 / (1.0 + jnp.exp(-z))
        h_ref[at, :] = (z * s).astype(BF16)
        dz_ref[at, :] = (acc_ref[at, :] * s * (1.0 + z * (1.0 - s))).astype(BF16)
        return carry

    lax.fori_loop(0, local // step, body, 0)
    weight_grad(full_ref, p_ref, dz_ref)
    scatter_grad(tab_ref, full_ref, (keep_ref, send_ref))

    def routes(p, carry):
        route_ref[rows(2 * p, piece), :] = h_ref[rows(sel_ref[p], piece), :]
        route_ref[rows(2 * p + 1, piece), :] = acc_ref[pl.ds(local + p * piece, piece), :].astype(BF16)
        return carry

    lax.fori_loop(0, peers, routes, 0)


def second_kernel(
    src_ref, tab_ref, h_ref, rim_ref, tile_ref, og_ref, w_ref, out_ref, keep_ref, send_ref, table_ref, p_ref, full_ref
):
    blocks, edge = tile_ref.shape[0], tile_ref.shape[2]
    fill_table(table_ref, h_ref, rim_ref)

    def body(i, carry):
        at = rows(i, edge)
        agg = aggregate_block(i, src_ref, tile_ref, table_ref)
        p_ref[at, :] = agg
        out_ref[at, :] = dot(agg, w_ref[...]).astype(BF16)
        return carry

    lax.fori_loop(0, blocks, body, 0)
    weight_grad(full_ref, p_ref, og_ref)
    scatter_grad(tab_ref, full_ref, (keep_ref, send_ref))


def place_kernel(tab_ref, *refs):
    parts, out_ref, sems = refs[:-2], refs[-2], refs[-1]
    count = tab_ref.shape[0]
    layers = out_ref.shape[0]
    per = len(parts) // layers
    half = count // per
    size = out_ref.shape[1] // count
    copies = []
    for layer in range(layers):
        for r in range(count):
            src = parts[layer * per + r // half]
            at = (r % half) * size
            copies.append(
                pltpu.make_async_copy(
                    src.at[pl.ds(at, size), :],
                    out_ref.at[layer, rows(tab_ref[r], size), :],
                    sems.at[layer * count + r],
                )
            )
    for c in copies:
        c.start()
    for c in copies:
        c.wait()


def call(body, out_shape, specs, out_specs, scratch, flops, moved, name):
    return pl.pallas_call(
        body,
        out_shape=out_shape,
        in_specs=specs,
        out_specs=out_specs,
        scratch_shapes=scratch,
        cost_estimate=pl.CostEstimate(flops=flops, bytes_accessed=moved, transcendentals=0),
        compiler_params=pltpu.CompilerParams(vmem_limit_bytes=40 * 1024 * 1024),
        name=name,
    )


def per_device(
    features,
    tile_src,
    tile_val,
    send_sel,
    stale_features,
    stale_grads,
    out_grad,
    master,
    moment_first,
    moment_second,
):
    peers = lax.axis_size("dom")
    groups = lax.axis_size("grp")
    devices = peers * groups
    local, width = features.shape
    total_nodes = local * devices
    blocks, tiles, edge = tile_val.shape[:3]
    rim = stale_features.shape[0]
    piece = rim // peers
    shard_rows = master.shape[1]
    full_rows = shard_rows * devices
    selects = send_sel[0]
    stages = plan_stages(peers, groups)
    order = relative_order(stages)
    masks = np.array(order, np.int32)
    owner = (lax.axis_index("dom") ^ masks[:, 0]) * groups + (lax.axis_index("grp") ^ masks[:, 1])
    packed = shard_rows % PACK == 0
    table = owner if packed else jnp.arange(full_rows // PACK, dtype=jnp.int32)
    half = full_rows // 2
    sds = jax.ShapeDtypeStruct

    def natural(parts):
        whole = jnp.concatenate(parts, 0).reshape(devices, shard_rows, width)
        inverse = jnp.argmax(owner[None, :] == jnp.arange(devices, dtype=jnp.int32)[:, None], axis=1)
        return jnp.take(whole, inverse, axis=0).reshape(full_rows, width)

    def relative(parts):
        whole = jnp.concatenate(parts, 0).reshape(devices, shard_rows, width)
        ordered = jnp.take(whole, owner, axis=0).reshape(full_rows, width)
        return ordered[:half], ordered[half:]

    def gather_weights(shard):
        parts = gather_relative(shard, stages)
        if not packed:
            whole = natural(parts)
            parts = (whole[:half], whole[half:])
        return parts

    def reduce_grad(keep, send):
        if not packed:
            keep, send = relative((keep, send))
        return reduce_relative(keep, send, stages) / total_nodes

    rounded = master.astype(BF16)
    picked = call(
        functools.partial(pick_kernel, piece, peers),
        sds((rim, width), BF16),
        [SMEM, ANY],
        VMEM,
        [pltpu.SemaphoreType.DMA((peers,))],
        0,
        rim * width * 4,
        "pick",
    )(selects, features)
    raw_rim = lax.all_to_all(picked.reshape(peers, piece, width), "dom", split_axis=0, concat_axis=0, tiled=True)
    raw_rim = raw_rim.reshape(rim, width)
    second_parts = gather_weights(rounded[1])
    first_parts = gather_weights(rounded[0])

    tile_flops = 2 * blocks * tiles * edge * edge * width
    dense_flops = 2 * local * width * width
    tile_bytes = tile_val.size * 2
    node_bytes = features.size * 2
    p_first = call(
        first_kernel,
        sds((local, width), BF16),
        [SMEM, VMEM, VMEM, VMEM],
        VMEM,
        [pltpu.VMEM((local + rim, width), BF16)],
        tile_flops,
        tile_bytes + 2 * node_bytes,
        "first",
    )(tile_src, features, raw_rim, tile_val)
    acc, w_second = call(
        spread_kernel,
        (sds((local + rim, width), F32), sds((full_rows, width), BF16)),
        [SMEM, SMEM, SMEM, VMEM, VMEM, VMEM, VMEM, VMEM],
        (VMEM, VMEM),
        [],
        tile_flops + dense_flops,
        tile_bytes + 3 * node_bytes,
        "spread",
    )(tile_src, selects, table, out_grad, tile_val, *second_parts, stale_grads)
    h_first, route, keep_first, send_first = call(
        hidden_kernel,
        (
            sds((local, width), BF16),
            sds((2 * rim, width), BF16),
            sds((half, width), BF16),
            sds((half, width), BF16),
        ),
        [SMEM, SMEM, VMEM, VMEM, VMEM, VMEM],
        (VMEM, VMEM, VMEM, VMEM),
        [
            pltpu.VMEM((full_rows, width), BF16),
            pltpu.VMEM((local, width), BF16),
            pltpu.VMEM((full_rows, width), F32),
        ],
        2 * dense_flops,
        4 * node_bytes,
        "hidden",
    )(selects, table, p_first, acc, *first_parts)
    g_first = reduce_grad(keep_first, send_first)
    layer_out, keep_second, send_second = call(
        second_kernel,
        (sds((local, width), BF16), sds((half, width), BF16), sds((half, width), BF16)),
        [SMEM, SMEM, VMEM, VMEM, VMEM, VMEM, VMEM],
        (VMEM, VMEM, VMEM),
        [
            pltpu.VMEM((local + rim, width), BF16),
            pltpu.VMEM((local, width), BF16),
            pltpu.VMEM((full_rows, width), F32),
        ],
        tile_flops + 2 * dense_flops,
        tile_bytes + 3 * node_bytes,
        "second",
    )(tile_src, table, h_first, stale_features, tile_val, out_grad, w_second)
    g_second = reduce_grad(keep_second, send_second)
    fresh = lax.all_to_all(route.reshape(peers, 2 * piece, width), "dom", split_axis=0, concat_axis=0, tiled=True)
    fresh_features = fresh[:, :piece].reshape(rim, width)
    fresh_grads = fresh[:, piece:].reshape(rim, width)

    nexts, parts = [], []
    for layer, shard in enumerate((g_first, g_second)):
        moment_new = decay_first * moment_first[layer] + (1.0 - decay_first) * shard
        second_new = decay_second * moment_second[layer] + (1.0 - decay_second) * shard * shard
        update = (
            moment_new
            / (1.0 - decay_first**STEP)
            / (jnp.sqrt(second_new / (1.0 - decay_second**STEP)) + epsilon)
        )
        moved = master[layer] - learn_rate * update
        nexts.append(moved)
        parts.append(gather_relative(moved.astype(BF16), stages))
    master_next = jnp.stack(nexts)
    if packed:
        weights_next = call(
            place_kernel,
            sds((2, full_rows, width), BF16),
            [SMEM, VMEM, VMEM, VMEM, VMEM],
            ANY,
            [pltpu.SemaphoreType.DMA((2 * devices,))],
            0,
            8 * full_rows * width,
            "place",
        )(table, *parts[0], *parts[1])
    else:
        weights_next = jnp.stack([natural(parts[0]), natural(parts[1])])
    return (layer_out, fresh_features, fresh_grads, master_next, weights_next)


def solution(mesh):
    placed = (
        P(("dom", "grp"), None),
        P(("dom", "grp"), None),
        P(("dom", "grp"), None, None, None),
        P(("dom", "grp"), None),
        P(("dom", "grp"), None),
        P(("dom", "grp"), None),
        P(("dom", "grp"), None),
        P(None, ("dom", "grp"), None),
        P(None, ("dom", "grp"), None),
        P(None, ("dom", "grp"), None),
    )
    return jax.shard_map(
        per_device,
        mesh=mesh,
        in_specs=placed,
        out_specs=(
            P(("dom", "grp"), None),
            P(("dom", "grp"), None),
            P(("dom", "grp"), None),
            P(None, ("dom", "grp"), None),
            P(),
        ),
        check_vma=False,
    )
```

```python
import functools

import jax
import jax.numpy as jnp
import numpy as np
from jax import lax
from jax.experimental import pallas as pl
from jax.experimental.pallas import tpu as pltpu
from jax.sharding import PartitionSpec as P

STEP = 10


decay_first = 0.9
decay_second = 0.95
learn_rate = 0.01
epsilon = 1e-08

F32 = jnp.float32
BF16 = jnp.bfloat16
AXES = ("dom", "grp")
VMEM = pl.BlockSpec(memory_space=pltpu.VMEM)
SMEM = pl.BlockSpec(memory_space=pltpu.SMEM)
ANY = pl.BlockSpec(memory_space=pl.ANY)
PACK = 16
LAYERS = 2
GROUP = 4


def plan_stages(nd, ng):
    dom_bits = [1 << i for i in range(nd.bit_length() - 1)]
    grp_bits = [1 << i for i in range(ng.bit_length() - 1)]
    groups = [[(0, b) for b in grp_bits[:1]], [(a, 0) for a in dom_bits[:1]] + [(0, b) for b in grp_bits[1:2]]]
    rest = [(a, 0) for a in dom_bits[1:]] + [(0, b) for b in grp_bits[2:]]
    groups += [rest[i : i + 2] for i in range(0, len(rest), 2)]
    stages = []
    for bits in groups:
        members = [(0, 0)]
        for a, b in bits:
            members = members + [(a ^ x, b ^ y) for x, y in members]
        if len(members) > 1:
            stages.append(members)
    return stages


def relative_order(stages):
    order = [(0, 0)]
    for members in stages:
        order = [(a ^ x, b ^ y) for a, b in order for x, y in members]
    return order


def swap(x, mask):
    nd, ng = lax.axis_size("dom"), lax.axis_size("grp")
    pairs = [(k, ((k // ng) ^ mask[0]) * ng + ((k % ng) ^ mask[1])) for k in range(nd * ng)]
    return lax.ppermute(x, AXES, pairs)


def gather_relative(shard, stages):
    held = shard
    for members in stages[:0:-1]:
        held = jnp.concatenate([held] + [swap(held, m) for m in members[1:]], 0)
    return held, swap(held, stages[0][1])


def reduce_relative(keep, send, stages):
    got = swap(send, stages[0][1])
    total = keep.astype(F32) + got.astype(F32)
    for members in stages[1:]:
        pieces = jnp.split(total.astype(BF16), len(members), 0)
        got = [swap(p, m) for p, m in zip(pieces[1:], members[1:])]
        total = pieces[0].astype(F32)
        for g in got:
            total = total + g.astype(F32)
    return total


def dom_stages(stages):
    split = [[m for m in members if m[1] == 0] for members in stages]
    return [members for members in split if len(members) > 1]


def exchange(parts, stages, turn):
    sizes = [len(members) for members in stages]
    places = list(np.ndindex(*sizes))
    held = dict(zip(places, parts))
    for s in turn:
        for i in range(1, sizes[s]):
            lanes = [at for at in places if at[s] == i]
            got = swap(jnp.concatenate([held[at] for at in lanes], 0), stages[s][i])
            held.update(zip(lanes, jnp.split(got, len(lanes), 0)))
    return [held[at] for at in places]


def dot(a, b, ca=1, cb=0):
    return lax.dot_general(a, b, (((ca,), (cb,)), ((), ())), preferred_element_type=F32)


def rows(start, size):
    return pl.ds(pl.multiple_of(start * size, size), size)


def run_copies(copies):
    for c in copies:
        c.start()
    for c in copies:
        c.wait()


def pick_kernel(piece, sel_ref, peer_ref, rows_ref, out_ref, sems):
    copies = []
    for r in range(peer_ref.shape[0]):
        src = rows_ref.at[rows(sel_ref[peer_ref[r]], piece), :]
        copies.append(pltpu.make_async_copy(src, out_ref.at[pl.ds(r * piece, piece), :], sems.at[r]))
    run_copies(copies)


def prepare_kernel(src_ref, tile_ref, turned_ref, list_ref, goal_ref, count_ref):
    blocks, tiles = tile_ref.shape[:2]
    total = blocks * tiles
    slots = count_ref.shape[0]
    groups = goal_ref.shape[0]

    def turn(i, carry):
        for t in range(tiles):
            turned_ref[i * tiles + t] = tile_ref[i, t].T
        return carry

    lax.fori_loop(0, blocks, turn, 0)
    turned_ref[total] = jnp.zeros_like(turned_ref[total])
    for b in range(slots):
        count_ref[b] = 0

    def clear(k, carry):
        list_ref[k] = total
        return carry

    lax.fori_loop(0, groups * GROUP, clear, 0)

    def tally(i, carry):
        for t in range(tiles):
            b = src_ref[i, t]
            count_ref[b] = count_ref[b] + 1
        return carry

    lax.fori_loop(0, blocks, tally, 0)
    first = jnp.int32(0)
    for b in range(slots):
        need = (count_ref[b] + (GROUP - 1)) // GROUP

        def mark(g, carry, b=b):
            goal_ref[g] = b
            return carry

        lax.fori_loop(first, first + need, mark, 0)
        count_ref[b] = first * GROUP
        first = first + need

    def rest(g, carry):
        goal_ref[g] = 0
        return carry

    lax.fori_loop(first, groups, rest, 0)
    goal_ref[groups - 1] = first

    def enter(i, carry):
        for t in range(tiles):
            b = src_ref[i, t]
            at = count_ref[b]
            list_ref[at] = i * tiles + t
            count_ref[b] = at + 1
        return carry

    lax.fori_loop(0, blocks, enter, 0)


def aggregate_block(i, src_ref, tile_ref, table_ref):
    tiles, edge = tile_ref.shape[1], tile_ref.shape[2]
    left = jnp.concatenate([tile_ref[i, t] for t in range(tiles)], 1)
    right = jnp.concatenate([table_ref[rows(src_ref[i, t], edge), :] for t in range(tiles)], 0)
    return dot(left, right).astype(BF16)


def first_kernel(src_ref, peer_ref, feat_ref, rim_ref, tile_ref, out_ref, turned_ref, table_ref):
    blocks, edge = tile_ref.shape[0], tile_ref.shape[2]
    local = feat_ref.shape[0]
    peers = peer_ref.shape[0]
    piece = rim_ref.shape[0] // peers
    table_ref[:local, :] = feat_ref[...]
    for r in range(peers):
        at = pl.multiple_of(local + peer_ref[r] * piece, piece)
        table_ref[pl.ds(at, piece), :] = rim_ref[r * piece : (r + 1) * piece, :]
    for i in range(blocks):
        out = aggregate_block(i, src_ref, tile_ref, table_ref)
        out_ref[i * edge : (i + 1) * edge, :] = out
        turned_ref[:, i * edge : (i + 1) * edge] = out.T


def assemble(dst_ref, tab_ref, parts, layer):
    count = tab_ref.shape[0]
    size = dst_ref.shape[0] // count
    half = count // len(parts)
    for r in range(count):
        at = ((r % half) * LAYERS + layer) * size
        dst_ref[rows(tab_ref[r], size), :] = parts[r // half][at : at + size, :]


def scatter_grad(tab_ref, full_ref, outs, layer):
    count = tab_ref.shape[0]
    size = full_ref.shape[0] // count
    half = count // len(outs)
    for r in range(count):
        at = ((r % half) * LAYERS + layer) * size
        outs[r // half][at : at + size, :] = full_ref[rows(tab_ref[r], size), :].astype(BF16)


def spread_kernel(list_ref, goal_ref, sel_ref, tab_ref, og_ref, turned_ref, lo_ref, hi_ref, stale_ref, acc_ref, w_ref, up_ref):
    edge = turned_ref.shape[1]
    blocks = og_ref.shape[0] // edge
    tiles = (turned_ref.shape[0] - 1) // blocks
    peers = sel_ref.shape[0]
    piece = stale_ref.shape[0] // peers
    assemble(w_ref, tab_ref, (lo_ref, hi_ref), 1)
    acc_ref[...] = jnp.zeros_like(acc_ref)
    step = 2 * edge

    def raise_rows(i, carry):
        up_ref[rows(i, step), :] = dot(og_ref[rows(i, step), :], w_ref[...], 1, 1).astype(BF16)
        return carry

    lax.fori_loop(0, blocks // 2, raise_rows, 0)

    def body(g, carry):
        ks = [list_ref[g * GROUP + j] for j in range(GROUP)]
        left = jnp.concatenate([turned_ref[k] for k in ks], 1)
        right = jnp.concatenate([up_ref[rows(jnp.minimum(k // tiles, blocks - 1), edge), :] for k in ks], 0)
        acc_ref[rows(goal_ref[g], edge), :] += dot(left, right)
        return carry

    lax.fori_loop(0, goal_ref[goal_ref.shape[0] - 1], body, 0)

    def place(p, carry):
        at = rows(sel_ref[p], piece)
        acc_ref[at, :] += stale_ref[rows(p, piece), :].astype(F32)
        return carry

    lax.fori_loop(0, peers, place, 0)


def hidden_kernel(
    sel_ref, peer_ref, tab_ref, p_ref, turned_ref, acc_ref, lo_ref, hi_ref, h_ref, route_ref, full_ref, w_ref, dz_ref
):
    step = 128
    local = p_ref.shape[0]
    peers = sel_ref.shape[0]
    piece = (acc_ref.shape[0] - local) // peers
    assemble(w_ref, tab_ref, (lo_ref, hi_ref), 0)

    def body(i, carry):
        at = rows(i, step)
        z = dot(p_ref[at, :], w_ref[...])
        s = 1.0 / (1.0 + jnp.exp(-z))
        h_ref[at, :] = (z * s).astype(BF16)
        dz_ref[at, :] = (acc_ref[at, :] * s * (1.0 + z * (1.0 - s))).astype(BF16)
        return carry

    lax.fori_loop(0, local // step, body, 0)
    for m in range(full_ref.shape[0] // step):
        at = slice(m * step, (m + 1) * step)
        full_ref[at, :] = dot(turned_ref[at, :], dz_ref[...])
    for r in range(peers):
        q = peer_ref[r]
        at = 2 * r * piece
        route_ref[at : at + piece, :] = h_ref[rows(sel_ref[q], piece), :]
        back = acc_ref[pl.ds(pl.multiple_of(local + q * piece, piece), piece), :]
        route_ref[at + piece : at + 2 * piece, :] = back.astype(BF16)


def second_kernel(src_ref, tab_ref, h_ref, rim_ref, tile_ref, og_ref, first_ref, p_ref, keep_ref, send_ref, table_ref, full_ref):
    blocks, edge = tile_ref.shape[0], tile_ref.shape[2]
    step = 128
    local = h_ref.shape[0]
    table_ref[:local, :] = h_ref[...]
    table_ref[local:, :] = rim_ref[...]

    def body(i, carry):
        p_ref[rows(i, edge), :] = aggregate_block(i, src_ref, tile_ref, table_ref)
        return carry

    lax.fori_loop(0, blocks, body, 0)
    for m in range(full_ref.shape[0] // step):
        cols = slice(m * step, (m + 1) * step)
        full_ref[cols, :] = dot(p_ref[:, cols], og_ref[...], 0, 0)
    scatter_grad(tab_ref, first_ref, (keep_ref, send_ref), 0)
    scatter_grad(tab_ref, full_ref, (keep_ref, send_ref), 1)


def out_kernel(p_ref, lo_ref, hi_ref, tab_ref, out_ref, w_ref):
    step = 128
    assemble(w_ref, tab_ref, (lo_ref, hi_ref), 1)

    def body(i, carry):
        out_ref[rows(i, step), :] = dot(p_ref[rows(i, step), :], w_ref[...]).astype(BF16)
        return carry

    lax.fori_loop(0, p_ref.shape[0] // step, body, 0)


def place_kernel(tab_ref, peer_ref, lo_ref, hi_ref, fresh_ref, out_ref, feat_ref, grad_ref, sems):
    parts = (lo_ref, hi_ref)
    count, peers = tab_ref.shape[0], peer_ref.shape[0]
    half = count // 2
    size = out_ref.shape[1] // count
    piece = feat_ref.shape[0] // peers
    copies = []

    def add(src, dst):
        copies.append(pltpu.make_async_copy(src, dst, sems.at[len(copies)]))

    for r in range(count):
        for layer in range(LAYERS):
            at = ((r % half) * LAYERS + layer) * size
            add(parts[r // half].at[pl.ds(at, size), :], out_ref.at[layer, rows(tab_ref[r], size), :])
    for r in range(peers):
        at = rows(peer_ref[r], piece)
        add(fresh_ref.at[pl.ds(2 * r * piece, piece), :], feat_ref.at[at, :])
        add(fresh_ref.at[pl.ds((2 * r + 1) * piece, piece), :], grad_ref.at[at, :])
    run_copies(copies)


def call(body, out_shape, specs, out_specs, scratch, flops, moved, name):
    return pl.pallas_call(
        body,
        out_shape=out_shape,
        in_specs=specs,
        out_specs=out_specs,
        scratch_shapes=scratch,
        cost_estimate=pl.CostEstimate(flops=flops, bytes_accessed=moved, transcendentals=0),
        compiler_params=pltpu.CompilerParams(vmem_limit_bytes=40 * 1024 * 1024),
        name=name,
    )


def per_device(
    features,
    tile_src,
    tile_val,
    send_sel,
    stale_features,
    stale_grads,
    out_grad,
    master,
    moment_first,
    moment_second,
):
    peers = lax.axis_size("dom")
    groups = lax.axis_size("grp")
    devices = peers * groups
    local, width = features.shape
    total_nodes = local * devices
    blocks, tiles, edge = tile_val.shape[:3]
    rim = stale_features.shape[0]
    piece = rim // peers
    layers, shard_rows = master.shape[:2]
    full_rows = shard_rows * devices
    slots = blocks + rim // edge
    selects = send_sel[0]
    stages = plan_stages(peers, groups)
    ways = dom_stages(stages)
    masks = np.array(relative_order(stages), np.int32)
    here = lax.axis_index("dom")
    owner = (here ^ masks[:, 0]) * groups + (lax.axis_index("grp") ^ masks[:, 1])
    peer = here ^ np.array(relative_order(ways), np.int32)[:, 0]
    packed = shard_rows % PACK == 0
    count = devices if packed else full_rows // PACK
    size = full_rows // count
    table = owner if packed else jnp.arange(count, dtype=jnp.int32)
    half = layers * full_rows // 2
    sds = jax.ShapeDtypeStruct

    def natural(parts):
        whole = jnp.concatenate(parts, 0).reshape(devices, layers, shard_rows, width)
        inverse = jnp.argmax(owner[None, :] == jnp.arange(devices, dtype=jnp.int32)[:, None], axis=1)
        return jnp.take(whole, inverse, axis=0).transpose(1, 0, 2, 3).reshape(layers, full_rows, width)

    def gather_weights(shard):
        parts = gather_relative(shard.reshape(layers * shard_rows, width), stages)
        if not packed:
            whole = natural(parts).reshape(layers, count, size, width).transpose(1, 0, 2, 3)
            whole = whole.reshape(layers * full_rows, width)
            parts = (whole[:half], whole[half:])
        return parts

    def reduce_grads(keep, send):
        if not packed:
            whole = jnp.concatenate((keep, send), 0).reshape(count, layers, size, width).transpose(1, 0, 2, 3)
            whole = whole.reshape(layers, devices, shard_rows, width).transpose(1, 0, 2, 3)
            whole = jnp.take(whole, owner, axis=0).reshape(layers * full_rows, width)
            keep, send = whole[:half], whole[half:]
        return reduce_relative(keep, send, stages).reshape(layers, shard_rows, width) / total_nodes

    tile_flops = 2 * blocks * tiles * edge * edge * width
    dense_flops = 2 * local * width * width
    tile_bytes = tile_val.size * 2
    node_bytes = features.size * 2
    nodes = sds((local, width), BF16)
    square = sds((full_rows, width), F32)
    grads_half = sds((half, width), BF16)
    listed = -(-(blocks * tiles + slots * (GROUP - 1)) // GROUP) + 1

    lo, hi = gather_weights(master.astype(BF16))
    picked = call(
        functools.partial(pick_kernel, piece),
        sds((rim, width), BF16),
        [SMEM, SMEM, ANY],
        VMEM,
        [pltpu.SemaphoreType.DMA((peers,))],
        0,
        rim * width * 4,
        "pick",
    )(selects, peer, features)
    raw_rim = jnp.concatenate(exchange(jnp.split(picked, peers, 0), ways, range(len(ways))), 0)
    turned_tiles, order, goal = call(
        prepare_kernel,
        (
            sds((blocks * tiles + 1, edge, edge), BF16),
            sds((listed * GROUP,), jnp.int32),
            sds((listed,), jnp.int32),
        ),
        [SMEM, VMEM],
        (VMEM, SMEM, SMEM),
        [pltpu.SMEM((slots,), jnp.int32)],
        0,
        2 * tile_bytes,
        "prepare",
    )(tile_src, tile_val)
    p_first, p_turned = call(
        first_kernel,
        (nodes, sds((width, local), BF16)),
        [SMEM, SMEM, VMEM, VMEM, VMEM],
        (VMEM, VMEM),
        [pltpu.VMEM((local + rim, width), BF16)],
        tile_flops,
        tile_bytes + 2 * node_bytes,
        "first",
    )(tile_src, peer, features, raw_rim, tile_val)
    acc = call(
        spread_kernel,
        sds((local + rim, width), F32),
        [SMEM, SMEM, SMEM, SMEM, VMEM, VMEM, VMEM, VMEM, VMEM],
        VMEM,
        [pltpu.VMEM((full_rows, width), BF16), pltpu.VMEM((local, width), BF16)],
        tile_flops + dense_flops,
        tile_bytes + 3 * node_bytes,
        "spread",
    )(order, goal, selects, table, out_grad, turned_tiles, lo, hi, stale_grads)
    h_first, route, g_first = call(
        hidden_kernel,
        (nodes, sds((2 * rim, width), BF16), square),
        [SMEM, SMEM, SMEM, VMEM, VMEM, VMEM, VMEM, VMEM],
        (VMEM, VMEM, VMEM),
        [pltpu.VMEM((full_rows, width), BF16), pltpu.VMEM((local, width), BF16)],
        2 * dense_flops,
        4 * node_bytes,
        "hidden",
    )(selects, peer, table, p_first, p_turned, acc, lo, hi)
    p_second, keep, send = call(
        second_kernel,
        (nodes, grads_half, grads_half),
        [SMEM, SMEM, VMEM, VMEM, VMEM, VMEM, VMEM],
        (VMEM, VMEM, VMEM),
        [pltpu.VMEM((local + rim, width), BF16), pltpu.VMEM((full_rows, width), F32)],
        tile_flops + dense_flops,
        tile_bytes + 3 * node_bytes,
        "second",
    )(tile_src, table, h_first, stale_features, tile_val, out_grad, g_first)
    shard = reduce_grads(keep, send)
    layer_out = call(
        out_kernel,
        nodes,
        [VMEM, VMEM, VMEM, SMEM],
        VMEM,
        [pltpu.VMEM((full_rows, width), BF16)],
        dense_flops,
        2 * node_bytes,
        "out",
    )(p_second, lo, hi, table)
    fresh = jnp.concatenate(exchange(jnp.split(route, peers, 0), ways, range(len(ways))[::-1]), 0)

    moment_new = decay_first * moment_first + (1.0 - decay_first) * shard
    second_new = decay_second * moment_second + (1.0 - decay_second) * shard * shard
    update = (
        moment_new
        / (1.0 - decay_first**STEP)
        / (jnp.sqrt(second_new / (1.0 - decay_second**STEP)) + epsilon)
    )
    master_next = master - learn_rate * update
    parts = gather_weights(master_next.astype(BF16))
    weights_next, fresh_features, fresh_grads = call(
        place_kernel,
        (sds((layers, full_rows, width), BF16), sds((rim, width), BF16), sds((rim, width), BF16)),
        [SMEM, SMEM, VMEM, VMEM, VMEM],
        (ANY, ANY, ANY),
        [pltpu.SemaphoreType.DMA((layers * count + 2 * peers,))],
        0,
        4 * layers * full_rows * width,
        "place",
    )(table, peer, *parts, fresh)
    return (layer_out, fresh_features, fresh_grads, master_next, weights_next)


def solution(mesh):
    placed = (
        P(("dom", "grp"), None),
        P(("dom", "grp"), None),
        P(("dom", "grp"), None, None, None),
        P(("dom", "grp"), None),
        P(("dom", "grp"), None),
        P(("dom", "grp"), None),
        P(("dom", "grp"), None),
        P(None, ("dom", "grp"), None),
        P(None, ("dom", "grp"), None),
        P(None, ("dom", "grp"), None),
    )
    return jax.shard_map(
        per_device,
        mesh=mesh,
        in_specs=placed,
        out_specs=(
            P(("dom", "grp"), None),
            P(("dom", "grp"), None),
            P(("dom", "grp"), None),
            P(None, ("dom", "grp"), None),
            P(),
        ),
        check_vma=False,
    )
```

```python
import functools

import jax
import jax.numpy as jnp
import numpy as np
from jax import lax
from jax.experimental import pallas as pl
from jax.experimental.pallas import tpu as pltpu
from jax.sharding import PartitionSpec as P


STEP = 10


decay_first = 0.9
decay_second = 0.95
learn_rate = 0.01
epsilon = 1e-08

F32 = jnp.float32
BF16 = jnp.bfloat16
AXES = ("dom", "grp")
VMEM = pl.BlockSpec(memory_space=pltpu.VMEM)
SMEM = pl.BlockSpec(memory_space=pltpu.SMEM)
ANY = pl.BlockSpec(memory_space=pl.ANY)
HBM = pl.BlockSpec(memory_space=pltpu.HBM)
PACK = 16
LAYERS = 2
GROUP = 4
BATCH = 5


def plan_stages(nd, ng):
    dom_bits = [1 << i for i in range(nd.bit_length() - 1)]
    grp_bits = [1 << i for i in range(ng.bit_length() - 1)]
    groups = [[(0, b) for b in grp_bits[:1]], [(a, 0) for a in dom_bits[:1]] + [(0, b) for b in grp_bits[1:2]]]
    rest = [(a, 0) for a in dom_bits[1:]] + [(0, b) for b in grp_bits[2:]]
    groups += [rest[i : i + 2] for i in range(0, len(rest), 2)]
    stages = []
    for bits in groups:
        members = [(0, 0)]
        for a, b in bits:
            members = members + [(a ^ x, b ^ y) for x, y in members]
        if len(members) > 1:
            stages.append(members)
    return stages


def relative_order(stages):
    order = [(0, 0)]
    for members in stages:
        order = [(a ^ x, b ^ y) for a, b in order for x, y in members]
    return order


def swap(x, mask):
    nd, ng = lax.axis_size("dom"), lax.axis_size("grp")
    pairs = [(k, ((k // ng) ^ mask[0]) * ng + ((k % ng) ^ mask[1])) for k in range(nd * ng)]
    return lax.ppermute(x, AXES, pairs)


def gather_relative(shard, stages, parts=(), ways=()):
    places = list(np.ndindex(*[len(members) for members in ways]))
    pieces = dict(zip(places, parts))
    held = shard
    for members in stages[:0:-1]:
        size = held.shape[0]
        got = [held]
        for m in members[1:]:
            lanes = [at for at in pieces for w, way in enumerate(ways) if m in way and at[w] == way.index(m)]
            came = swap(jnp.concatenate([held] + [pieces[at] for at in lanes], 0), m)
            got.append(came[:size])
            if lanes:
                pieces.update(zip(lanes, jnp.split(came[size:], len(lanes), 0)))
        held = jnp.concatenate(got, 0)
    other = swap(held, stages[0][1])
    return held, other, [pieces[at] for at in pieces]


def reduce_relative(keep, send, stages):
    got = swap(send, stages[0][1])
    total = keep.astype(F32) + got.astype(F32)
    for members in stages[1:]:
        pieces = jnp.split(total.astype(BF16), len(members), 0)
        got = [swap(p, m) for p, m in zip(pieces[1:], members[1:])]
        total = pieces[0].astype(F32)
        for g in got:
            total = total + g.astype(F32)
    return total


def dom_stages(stages):
    split = [[m for m in members if m[1] == 0] for members in stages]
    return [members for members in split if len(members) > 1]


def exchange(parts, ways, turn):
    places = list(np.ndindex(*[len(members) for members in ways]))
    held = dict(zip(places, parts))
    for s in turn:
        for i in range(1, len(ways[s])):
            lanes = [at for at in places if at[s] == i]
            got = swap(jnp.concatenate([held[at] for at in lanes], 0), ways[s][i])
            held.update(zip(lanes, jnp.split(got, len(lanes), 0)))
    return [held[at] for at in places]


class Layout:
    def __init__(self, nd, ng, shard_rows):
        self.stages = plan_stages(nd, ng)
        self.ways = dom_stages(self.stages)
        self.blocks = relative_order(self.stages)
        self.peers = [a for a, _ in relative_order(self.ways)]
        self.ng = ng
        self.packed = shard_rows % PACK == 0
        self.count = nd * ng if self.packed else nd * ng * shard_rows // PACK

    def owner(self, r):
        a, b = self.blocks[r]
        return (lax.axis_index("dom") ^ a) * self.ng + (lax.axis_index("grp") ^ b)

    def block(self, r):
        return self.owner(r) if self.packed else r

    def peer(self, r):
        return lax.axis_index("dom") ^ self.peers[r]


def dot(a, b, ca=1, cb=0):
    return lax.dot_general(a, b, (((ca,), (cb,)), ((), ())), preferred_element_type=F32)


def rows(start, size):
    return pl.ds(pl.multiple_of(start * size, size), size)


def begin_kernel(lay, sel_hbm, master_hbm, rows_ref, own_ref, out_ref, sel_ref, master_ref, sems):
    peers = len(lay.peers)
    piece = out_ref.shape[0] // peers
    sel_copy = pltpu.make_async_copy(sel_hbm, sel_ref, sems.at[peers])
    master_copy = pltpu.make_async_copy(master_hbm, master_ref, sems.at[peers + 1])
    sel_copy.start()
    master_copy.start()
    sel_copy.wait()
    copies = []
    for r in range(peers):
        src = rows_ref.at[rows(sel_ref[0, lay.peer(r)], piece), :]
        copies.append(pltpu.make_async_copy(src, out_ref.at[pl.ds(r * piece, piece), :], sems.at[r]))
    for c in copies:
        c.start()
    master_copy.wait()
    own_ref[...] = master_ref[...].astype(BF16)
    for c in copies:
        c.wait()


def prepare_kernel(src_ref, tile_ref, turned_ref, list_ref, goal_ref, count_ref):
    blocks, tiles = tile_ref.shape[:2]
    total = blocks * tiles
    slots = count_ref.shape[0]
    groups = goal_ref.shape[0]

    def turn(i, carry):
        for t in range(tiles):
            turned_ref[i * tiles + t] = tile_ref[i, t].T
        return carry

    lax.fori_loop(0, blocks, turn, 0)
    turned_ref[total] = jnp.zeros_like(turned_ref[total])
    for b in range(slots):
        count_ref[b] = 0

    def clear(k, carry):
        list_ref[k] = total
        return carry

    lax.fori_loop(0, groups * GROUP, clear, 0)

    def tally(i, carry):
        for t in range(tiles):
            b = src_ref[i, t]
            count_ref[b] = count_ref[b] + 1
        return carry

    lax.fori_loop(0, blocks, tally, 0)
    first = jnp.int32(0)
    for b in range(slots):
        need = (count_ref[b] + (GROUP - 1)) // GROUP

        def mark(g, carry, b=b):
            goal_ref[g] = b
            return carry

        lax.fori_loop(first, first + need, mark, 0)
        count_ref[b] = first * GROUP
        first = first + need

    def rest(g, carry):
        goal_ref[g] = 0
        return carry

    lax.fori_loop(first, groups, rest, 0)
    goal_ref[groups - 1] = first

    def enter(i, carry):
        for t in range(tiles):
            b = src_ref[i, t]
            at = count_ref[b]
            list_ref[at] = i * tiles + t
            count_ref[b] = at + 1
        return carry

    lax.fori_loop(0, blocks, enter, 0)


def aggregate_block(i, src_ref, tile_ref, table_ref):
    tiles, edge = tile_ref.shape[1], tile_ref.shape[2]
    left = jnp.concatenate([tile_ref[i, t] for t in range(tiles)], 1)
    right = jnp.concatenate([table_ref[rows(src_ref[i, t], edge), :] for t in range(tiles)], 0)
    return dot(left, right).astype(BF16)


def first_kernel(lay, src_ref, feat_ref, rim_ref, tile_ref, out_ref, turned_ref, table_ref):
    blocks, edge = tile_ref.shape[0], tile_ref.shape[2]
    local = feat_ref.shape[0]
    peers = len(lay.peers)
    piece = rim_ref.shape[0] // peers
    table_ref[:local, :] = feat_ref[...]
    for r in range(peers):
        at = pl.multiple_of(local + lay.peer(r) * piece, piece)
        table_ref[pl.ds(at, piece), :] = rim_ref[r * piece : (r + 1) * piece, :]
    for i in range(blocks):
        out = aggregate_block(i, src_ref, tile_ref, table_ref)
        out_ref[i * edge : (i + 1) * edge, :] = out
        turned_ref[:, i * edge : (i + 1) * edge] = out.T


def assemble(lay, dst_ref, parts, layer):
    size = dst_ref.shape[0] // lay.count
    half = lay.count // len(parts)
    for r in range(lay.count):
        at = ((r % half) * LAYERS + layer) * size
        dst_ref[rows(lay.block(r), size), :] = parts[r // half][at : at + size, :]


def scatter_grad(lay, full_ref, outs, layer):
    size = full_ref.shape[0] // lay.count
    half = lay.count // len(outs)
    for r in range(lay.count):
        at = ((r % half) * LAYERS + layer) * size
        outs[r // half][at : at + size, :] = full_ref[rows(lay.block(r), size), :].astype(BF16)


def spread_kernel(lay, list_ref, goal_ref, sel_ref, og_ref, turned_ref, lo_ref, hi_ref, stale_ref, acc_ref, w_ref, up_ref):
    edge = turned_ref.shape[1]
    blocks = og_ref.shape[0] // edge
    tiles = (turned_ref.shape[0] - 1) // blocks
    peers = len(lay.peers)
    piece = stale_ref.shape[0] // peers
    assemble(lay, w_ref, (lo_ref, hi_ref), 1)
    acc_ref[...] = jnp.zeros_like(acc_ref)
    for i in range(blocks):
        at = slice(i * edge, (i + 1) * edge)
        up_ref[at, :] = dot(og_ref[at, :], w_ref[...], 1, 1).astype(BF16)

    def body(n, carry):
        sums = []
        for u in range(BATCH):
            g = n * BATCH + u
            ks = [list_ref[g * GROUP + j] for j in range(GROUP)]
            left = jnp.concatenate([turned_ref[k] for k in ks], 1)
            right = jnp.concatenate([up_ref[rows(jnp.minimum(k // tiles, blocks - 1), edge), :] for k in ks], 0)
            sums.append((rows(goal_ref[g], edge), dot(left, right)))
        for at, part in sums:
            acc_ref[at, :] += part
        return carry

    used = goal_ref[goal_ref.shape[0] - 1]
    lax.fori_loop(0, (used + (BATCH - 1)) // BATCH, body, 0)
    for p in range(peers):
        at = rows(sel_ref[p], piece)
        acc_ref[at, :] += stale_ref[p * piece : (p + 1) * piece, :].astype(F32)


def hidden_kernel(lay, sel_ref, p_ref, turned_ref, acc_ref, lo_ref, hi_ref, h_ref, route_ref, full_ref, w_ref, dz_ref):
    step = 128
    local = p_ref.shape[0]
    peers = len(lay.peers)
    piece = (acc_ref.shape[0] - local) // peers
    assemble(lay, w_ref, (lo_ref, hi_ref), 0)
    for i in range(local // step):
        at = slice(i * step, (i + 1) * step)
        z = dot(p_ref[at, :], w_ref[...])
        s = 1.0 / (1.0 + jnp.exp(-z))
        h_ref[at, :] = (z * s).astype(BF16)
        dz_ref[at, :] = (acc_ref[at, :] * s * (1.0 + z * (1.0 - s))).astype(BF16)
    for m in range(full_ref.shape[0] // step):
        at = slice(m * step, (m + 1) * step)
        full_ref[at, :] = dot(turned_ref[at, :], dz_ref[...])
    for r in range(peers):
        q = lay.peer(r)
        at = 2 * r * piece
        route_ref[at : at + piece, :] = h_ref[rows(sel_ref[q], piece), :]
        back = acc_ref[pl.ds(pl.multiple_of(local + q * piece, piece), piece), :]
        route_ref[at + piece : at + 2 * piece, :] = back.astype(BF16)


def second_kernel(lay, src_ref, h_ref, rim_ref, tile_ref, og_ref, first_ref, p_ref, keep_ref, send_ref, table_ref, full_ref):
    blocks, edge = tile_ref.shape[0], tile_ref.shape[2]
    step = 128
    local = h_ref.shape[0]
    table_ref[:local, :] = h_ref[...]
    table_ref[local:, :] = rim_ref[...]
    for i in range(blocks):
        p_ref[i * edge : (i + 1) * edge, :] = aggregate_block(i, src_ref, tile_ref, table_ref)
    for m in range(full_ref.shape[0] // step):
        cols = slice(m * step, (m + 1) * step)
        full_ref[cols, :] = dot(p_ref[:, cols], og_ref[...], 0, 0)
    scatter_grad(lay, first_ref, (keep_ref, send_ref), 0)
    scatter_grad(lay, full_ref, (keep_ref, send_ref), 1)


def out_kernel(lay, p_ref, lo_ref, hi_ref, out_ref, w_ref):
    step = 128
    assemble(lay, w_ref, (lo_ref, hi_ref), 1)
    for i in range(p_ref.shape[0] // step):
        at = slice(i * step, (i + 1) * step)
        out_ref[at, :] = dot(p_ref[at, :], w_ref[...]).astype(BF16)


def place_rows(lay, half_at, part_ref, out_ref):
    half = lay.count // 2
    size = out_ref.shape[1] // lay.count
    for r in range(half):
        for layer in range(LAYERS):
            src = part_ref.at[pl.ds((r * LAYERS + layer) * size, size), :]
            yield src, out_ref.at[layer, rows(lay.block(half_at * half + r), size), :]


def place_fresh(lay, fresh_ref, feat_ref, grad_ref):
    piece = feat_ref.shape[0] // len(lay.peers)
    for r in range(len(lay.peers)):
        at = rows(lay.peer(r), piece)
        yield fresh_ref.at[pl.ds(2 * r * piece, piece), :], feat_ref.at[at, :]
        yield fresh_ref.at[pl.ds((2 * r + 1) * piece, piece), :], grad_ref.at[at, :]


def run_copies(pairs, sems):
    copies = [pltpu.make_async_copy(src, dst, sems.at[n]) for n, (src, dst) in enumerate(pairs)]
    for c in copies:
        c.start()
    for c in copies:
        c.wait()


def place_kernel(lay, part_ref, fresh_ref, out_ref, feat_ref, grad_ref, sems):
    pairs = [*place_rows(lay, 0, part_ref, out_ref), *place_fresh(lay, fresh_ref, feat_ref, grad_ref)]
    run_copies(pairs, sems)


def finish_kernel(lay, part_ref, held_ref, out_ref, sems):
    run_copies(place_rows(lay, 1, part_ref, out_ref), sems)


def call(body, out_shape, specs, out_specs, scratch, flops, moved, aliases=None):
    return pl.pallas_call(
        body,
        out_shape=out_shape,
        in_specs=specs,
        out_specs=out_specs,
        scratch_shapes=scratch,
        input_output_aliases=aliases or {},
        cost_estimate=pl.CostEstimate(flops=flops, bytes_accessed=moved, transcendentals=0),
        compiler_params=pltpu.CompilerParams(vmem_limit_bytes=40 * 1024 * 1024),
    )


def epoch(
    features,
    tile_src,
    tile_val,
    send_sel,
    stale_features,
    stale_grads,
    out_grad,
    master,
    moment_first,
    moment_second,
):
    peers = lax.axis_size("dom")
    groups = lax.axis_size("grp")
    devices = peers * groups
    local, width = features.shape
    total_nodes = local * devices
    blocks, tiles, edge = tile_val.shape[:3]
    rim = stale_features.shape[0]
    layers, shard_rows = master.shape[:2]
    full_rows = shard_rows * devices
    slots = blocks + rim // edge
    selects = send_sel[0]
    lay = Layout(peers, groups, shard_rows)
    count, size = lay.count, full_rows // lay.count
    half = layers * full_rows // 2
    sds = jax.ShapeDtypeStruct

    def spread_out(lo, hi):
        if lay.packed:
            return lo, hi
        owner = jnp.stack([lay.owner(r) for r in range(devices)])
        inverse = jnp.argmax(owner[None, :] == jnp.arange(devices, dtype=jnp.int32)[:, None], axis=1)
        whole = jnp.concatenate((lo, hi), 0).reshape(devices, layers, shard_rows, width)
        whole = jnp.take(whole, inverse, axis=0).transpose(1, 0, 2, 3).reshape(layers, count, size, width)
        whole = whole.transpose(1, 0, 2, 3).reshape(layers * full_rows, width)
        return whole[:half], whole[half:]

    def draw_in(keep, send):
        if lay.packed:
            return keep, send
        owner = jnp.stack([lay.owner(r) for r in range(devices)])
        whole = jnp.concatenate((keep, send), 0).reshape(count, layers, size, width).transpose(1, 0, 2, 3)
        whole = whole.reshape(layers, devices, shard_rows, width).transpose(1, 0, 2, 3)
        whole = jnp.take(whole, owner, axis=0).reshape(layers * full_rows, width)
        return whole[:half], whole[half:]

    tile_flops = 2 * blocks * tiles * edge * edge * width
    dense_flops = 2 * local * width * width
    tile_bytes = tile_val.size * 2
    node_bytes = features.size * 2
    nodes = sds((local, width), BF16)
    square = sds((full_rows, width), F32)
    grads_half = sds((half, width), BF16)
    listed = -(-(blocks * tiles + slots * (GROUP - 1)) // GROUP)
    listed = -(-listed // BATCH) * BATCH + 1
    part = functools.partial

    own, picked = call(
        part(begin_kernel, lay),
        (sds(master.shape, BF16), sds((rim, width), BF16)),
        [HBM, HBM, HBM],
        (VMEM, VMEM),
        [
            pltpu.SMEM((1, peers), jnp.int32),
            pltpu.VMEM(master.shape, F32),
            pltpu.SemaphoreType.DMA((peers + 2,)),
        ],
        0,
        rim * width * 4,
    )(*(pltpu.with_memory_space_constraint(x, pltpu.HBM) for x in (send_sel, master, features)))
    lo, hi, raw_rim = gather_relative(
        own.reshape(layers * shard_rows, width), lay.stages, jnp.split(picked, peers, 0), lay.ways
    )
    lo, hi = spread_out(lo, hi)
    raw_rim = jnp.concatenate(raw_rim, 0)
    turned_tiles, order, goal = call(
        prepare_kernel,
        (
            sds((blocks * tiles + 1, edge, edge), BF16),
            sds((listed * GROUP,), jnp.int32),
            sds((listed,), jnp.int32),
        ),
        [SMEM, VMEM],
        (VMEM, SMEM, SMEM),
        [pltpu.SMEM((slots,), jnp.int32)],
        0,
        2 * tile_bytes,
    )(tile_src, tile_val)
    p_first, p_turned = call(
        part(first_kernel, lay),
        (nodes, sds((width, local), BF16)),
        [SMEM, VMEM, VMEM, VMEM],
        (VMEM, VMEM),
        [pltpu.VMEM((local + rim, width), BF16)],
        tile_flops,
        tile_bytes + 2 * node_bytes,
    )(tile_src, features, raw_rim, tile_val)
    acc = call(
        part(spread_kernel, lay),
        sds((local + rim, width), F32),
        [SMEM, SMEM, SMEM, VMEM, VMEM, VMEM, VMEM, VMEM],
        VMEM,
        [pltpu.VMEM((full_rows, width), BF16), pltpu.VMEM((local, width), BF16)],
        tile_flops + dense_flops,
        tile_bytes + 3 * node_bytes,
    )(order, goal, selects, out_grad, turned_tiles, lo, hi, stale_grads)
    h_first, route, g_first = call(
        part(hidden_kernel, lay),
        (nodes, sds((2 * rim, width), BF16), square),
        [SMEM, VMEM, VMEM, VMEM, VMEM, VMEM],
        (VMEM, VMEM, VMEM),
        [pltpu.VMEM((full_rows, width), BF16), pltpu.VMEM((local, width), BF16)],
        2 * dense_flops,
        4 * node_bytes,
    )(selects, p_first, p_turned, acc, lo, hi)
    p_second, keep, send = call(
        part(second_kernel, lay),
        (nodes, grads_half, grads_half),
        [SMEM, VMEM, VMEM, VMEM, VMEM, VMEM],
        (VMEM, VMEM, VMEM),
        [pltpu.VMEM((local + rim, width), BF16), pltpu.VMEM((full_rows, width), F32)],
        tile_flops + dense_flops,
        tile_bytes + 3 * node_bytes,
    )(tile_src, h_first, stale_features, tile_val, out_grad, g_first)
    shard = reduce_relative(*draw_in(keep, send), lay.stages).reshape(layers, shard_rows, width) / total_nodes
    layer_out = call(
        part(out_kernel, lay),
        nodes,
        [VMEM, VMEM, VMEM],
        VMEM,
        [pltpu.VMEM((full_rows, width), BF16)],
        dense_flops,
        2 * node_bytes,
    )(p_second, lo, hi)
    fresh = jnp.concatenate(exchange(jnp.split(route, peers, 0), lay.ways, range(len(lay.ways))[::-1]), 0)

    moment_new = decay_first * moment_first + (1.0 - decay_first) * shard
    second_new = decay_second * moment_second + (1.0 - decay_second) * shard * shard
    update = moment_new / (1.0 - decay_first**STEP) / (jnp.sqrt(second_new / (1.0 - decay_second**STEP)) + epsilon)
    master_next = master - learn_rate * update
    moved = master_next.astype(BF16).reshape(layers * shard_rows, width)
    lo_next, hi_next, _ = gather_relative(moved, lay.stages)
    lo_next, hi_next = spread_out(lo_next, hi_next)
    weights = sds((layers, full_rows, width), BF16)
    weights_next, fresh_features, fresh_grads = call(
        part(place_kernel, lay),
        (weights, sds((rim, width), BF16), sds((rim, width), BF16)),
        [VMEM, VMEM],
        (HBM, HBM, HBM),
        [pltpu.SemaphoreType.DMA((layers * count // 2 + 2 * peers,))],
        0,
        2 * layers * full_rows * width,
    )(lo_next, fresh)
    weights_next = call(
        part(finish_kernel, lay),
        weights,
        [VMEM, HBM],
        HBM,
        [pltpu.SemaphoreType.DMA((layers * count // 2,))],
        0,
        2 * layers * full_rows * width,
        aliases={1: 0},
    )(hi_next, weights_next)
    return (layer_out, fresh_features, fresh_grads, master_next, weights_next)


def solution(mesh):
    placed = (
        P(("dom", "grp"), None),
        P(("dom", "grp"), None),
        P(("dom", "grp"), None, None, None),
        P(("dom", "grp"), None),
        P(("dom", "grp"), None),
        P(("dom", "grp"), None),
        P(("dom", "grp"), None),
        P(None, ("dom", "grp"), None),
        P(None, ("dom", "grp"), None),
        P(None, ("dom", "grp"), None),
    )
    return jax.shard_map(
        epoch,
        mesh=mesh,
        in_specs=placed,
        out_specs=(
            P(("dom", "grp"), None),
            P(("dom", "grp"), None),
            P(("dom", "grp"), None),
            P(None, ("dom", "grp"), None),
            P(),
        ),
        check_vma=False,
    )
```

```python
import functools

import jax
import jax.numpy as jnp
import numpy as np
from jax import lax
from jax.experimental import pallas as pl
from jax.experimental.pallas import tpu as pltpu
from jax.sharding import PartitionSpec as P


STEP = 10


decay_first = 0.9
decay_second = 0.95
learn_rate = 0.01
epsilon = 1e-08

F32 = jnp.float32
BF16 = jnp.bfloat16
AXES = ("dom", "grp")
VMEM = pl.BlockSpec(memory_space=pltpu.VMEM)
SMEM = pl.BlockSpec(memory_space=pltpu.SMEM)
ANY = pl.BlockSpec(memory_space=pl.ANY)
HBM = pl.BlockSpec(memory_space=pltpu.HBM)
PACK = 16
LAYERS = 2
GROUP = 4
STRIP = 256


def plan_stages(nd, ng):
    dom_bits = [1 << i for i in range(nd.bit_length() - 1)]
    grp_bits = [1 << i for i in range(ng.bit_length() - 1)]
    groups = [[(0, b) for b in grp_bits[:1]], [(a, 0) for a in dom_bits[:1]] + [(0, b) for b in grp_bits[1:2]]]
    rest = [(a, 0) for a in dom_bits[1:]] + [(0, b) for b in grp_bits[2:]]
    groups += [rest[i : i + 2] for i in range(0, len(rest), 2)]
    stages = []
    for bits in groups:
        members = [(0, 0)]
        for a, b in bits:
            members = members + [(a ^ x, b ^ y) for x, y in members]
        if len(members) > 1:
            stages.append(members)
    return stages


def relative_order(stages):
    order = [(0, 0)]
    for members in stages:
        order = [(a ^ x, b ^ y) for a, b in order for x, y in members]
    return order


def swap(x, mask):
    nd, ng = lax.axis_size("dom"), lax.axis_size("grp")
    pairs = [(k, ((k // ng) ^ mask[0]) * ng + ((k % ng) ^ mask[1])) for k in range(nd * ng)]
    return lax.ppermute(x, AXES, pairs)


def gather_relative(shard, stages, parts=(), ways=()):
    places = list(np.ndindex(*[len(members) for members in ways]))
    pieces = dict(zip(places, parts))
    held = shard
    for members in stages[:0:-1]:
        size = held.shape[0]
        got = [held]
        for m in members[1:]:
            lanes = [at for at in pieces for w, way in enumerate(ways) if m in way and at[w] == way.index(m)]
            came = swap(jnp.concatenate([held] + [pieces[at] for at in lanes], 0), m)
            got.append(came[:size])
            if lanes:
                pieces.update(zip(lanes, jnp.split(came[size:], len(lanes), 0)))
        held = jnp.concatenate(got, 0)
    other = swap(held, stages[0][1])
    return held, other, [pieces[at] for at in pieces]


def reduce_relative(keep, send, stages):
    pieces = []
    for k, s in zip(*(jnp.split(x, len(stages[1]), 0) for x in (keep, send))):
        pieces.append((k.astype(F32) + swap(s, stages[0][1]).astype(F32)).astype(BF16))
    for n, members in enumerate(stages[1:]):
        if n:
            pieces = jnp.split(sum(t.astype(F32) for t in terms).astype(BF16), len(members), 0)
        terms = [pieces[0]] + [swap(p, m) for p, m in zip(pieces[1:], members[1:])]
    return terms


def dom_stages(stages):
    split = [[m for m in members if m[1] == 0] for members in stages]
    return [members for members in split if len(members) > 1]


def exchange(parts, ways, turn):
    places = list(np.ndindex(*[len(members) for members in ways]))
    held = dict(zip(places, parts))
    for s in turn:
        for i in range(1, len(ways[s])):
            lanes = [at for at in places if at[s] == i]
            got = swap(jnp.concatenate([held[at] for at in lanes], 0), ways[s][i])
            held.update(zip(lanes, jnp.split(got, len(lanes), 0)))
    return [held[at] for at in places]


class Layout:
    def __init__(self, nd, ng, shard_rows):
        self.stages = plan_stages(nd, ng)
        self.ways = dom_stages(self.stages)
        self.blocks = relative_order(self.stages)
        self.peers = [a for a, _ in relative_order(self.ways)]
        self.ng = ng
        self.packed = shard_rows % PACK == 0
        self.count = nd * ng if self.packed else nd * ng * shard_rows // PACK

    def owner(self, r):
        a, b = self.blocks[r]
        return (lax.axis_index("dom") ^ a) * self.ng + (lax.axis_index("grp") ^ b)

    def block(self, r):
        return self.owner(r) if self.packed else r

    def peer(self, r):
        return lax.axis_index("dom") ^ self.peers[r]


def dot(a, b, ca=1, cb=0):
    return lax.dot_general(a, b, (((ca,), (cb,)), ((), ())), preferred_element_type=F32)


def rows(start, size):
    return pl.ds(pl.multiple_of(start * size, size), size)


def strips(width):
    return [slice(n, n + STRIP) for n in range(0, width, STRIP)]


def begin_kernel(lay, sel_hbm, master_hbm, rows_ref, own_ref, out_ref, sel_ref, master_ref, sems):
    peers = len(lay.peers)
    piece = out_ref.shape[0] // peers
    sel_copy = pltpu.make_async_copy(sel_hbm, sel_ref, sems.at[peers])
    master_copy = pltpu.make_async_copy(master_hbm, master_ref, sems.at[peers + 1])
    sel_copy.start()
    master_copy.start()
    sel_copy.wait()
    copies = []
    for r in range(peers):
        src = rows_ref.at[rows(sel_ref[0, lay.peer(r)], piece), :]
        copies.append(pltpu.make_async_copy(src, out_ref.at[pl.ds(r * piece, piece), :], sems.at[r]))
    for c in copies:
        c.start()
    master_copy.wait()
    own_ref[...] = master_ref[...].astype(BF16)
    for c in copies:
        c.wait()


def prepare_kernel(src_ref, tile_hbm, turned_ref, list_ref, goal_ref, bound_ref, tile_ref, count_ref, sems):
    blocks, tiles = tile_ref.shape[:2]
    copies = [pltpu.make_async_copy(tile_hbm.at[i], tile_ref.at[i], sems.at[i]) for i in range(blocks)]
    for c in copies:
        c.start()
    total = blocks * tiles
    slots = count_ref.shape[0]
    groups = goal_ref.shape[0]

    turned_ref[total] = jnp.zeros_like(turned_ref[total])
    for b in range(slots):
        count_ref[b] = 0

    def clear(k, carry):
        list_ref[k] = total
        return carry

    lax.fori_loop(0, groups * GROUP, clear, 0)

    def tally(i, carry):
        for t in range(tiles):
            b = src_ref[i, t]
            count_ref[b] = count_ref[b] + 1
        return carry

    lax.fori_loop(0, blocks, tally, 0)
    first = jnp.int32(0)
    for b in range(slots):
        need = (count_ref[b] + (GROUP - 1)) // GROUP

        def mark(g, carry, b=b):
            goal_ref[g] = b
            return carry

        lax.fori_loop(first, first + need, mark, 0)
        count_ref[b] = first * GROUP
        if b == blocks:
            bound_ref[0] = first * GROUP
        first = first + need

    def rest(g, carry):
        goal_ref[g] = 0
        return carry

    lax.fori_loop(first, groups, rest, 0)
    bound_ref[1] = first * GROUP

    def enter(i, carry):
        for t in range(tiles):
            b = src_ref[i, t]
            at = count_ref[b]
            list_ref[at] = i * tiles + t
            count_ref[b] = at + 1
        return carry

    lax.fori_loop(0, blocks, enter, 0)
    for i in range(blocks):
        copies[i].wait()
        for t in range(tiles):
            turned_ref[i * tiles + t] = tile_ref[i, t].T


def aggregate_block(i, src_ref, tile_ref, table_ref):
    tiles, edge = tile_ref.shape[1], tile_ref.shape[2]
    left = jnp.concatenate([tile_ref[i, t] for t in range(tiles)], 1)
    right = jnp.concatenate([table_ref[rows(src_ref[i, t], edge), :] for t in range(tiles)], 0)
    return dot(left, right).astype(BF16)


def first_kernel(lay, src_ref, feat_ref, rim_ref, tile_ref, out_ref, turned_ref, table_ref):
    blocks, edge = tile_ref.shape[0], tile_ref.shape[2]
    local = feat_ref.shape[0]
    peers = len(lay.peers)
    piece = rim_ref.shape[0] // peers
    table_ref[:local, :] = feat_ref[...]
    for r in range(peers):
        at = pl.multiple_of(local + lay.peer(r) * piece, piece)
        table_ref[pl.ds(at, piece), :] = rim_ref[r * piece : (r + 1) * piece, :]
    for i in range(blocks):
        out = aggregate_block(i, src_ref, tile_ref, table_ref)
        out_ref[i * edge : (i + 1) * edge, :] = out
        turned_ref[:, i * edge : (i + 1) * edge] = out.T


def assemble(lay, dst_ref, parts, layer):
    size = dst_ref.shape[0] // lay.count
    half = lay.count // len(parts)
    for r in range(lay.count):
        at = ((r % half) * LAYERS + layer) * size
        dst_ref[rows(lay.block(r), size), :] = parts[r // half][at : at + size, :]


def scatter_grad(lay, full_ref, outs, layer):
    size = full_ref.shape[0] // lay.count
    half = lay.count // len(outs)
    for r in range(lay.count):
        at = ((r % half) * LAYERS + layer) * size
        outs[r // half][at : at + size, :] = full_ref[rows(lay.block(r), size), :].astype(BF16)


def spread_kernel(lay, list_ref, goal_ref, sel_ref, og_ref, turned_ref, lo_ref, hi_ref, stale_ref, acc_ref, w_ref, up_ref):
    edge = turned_ref.shape[1]
    blocks = og_ref.shape[0] // edge
    tiles = (turned_ref.shape[0] - 1) // blocks
    peers = len(lay.peers)
    piece = stale_ref.shape[0] // peers
    assemble(lay, w_ref, (lo_ref, hi_ref), 1)
    acc_ref[...] = jnp.zeros_like(acc_ref)
    for n in strips(w_ref.shape[0]):
        up_ref[:, n] = dot(og_ref[...], w_ref[n, :], 1, 1).astype(BF16)

    for g in range(goal_ref.shape[0]):
        ks = [list_ref[g * GROUP + j] for j in range(GROUP)]
        left = jnp.concatenate([turned_ref[k] for k in ks], 1)
        right = jnp.concatenate([up_ref[rows(jnp.minimum(k // tiles, blocks - 1), edge), :] for k in ks], 0)
        acc_ref[rows(goal_ref[g], edge), :] += dot(left, right)
    for p in range(peers):
        at = rows(sel_ref[p], piece)
        acc_ref[at, :] += stale_ref[p * piece : (p + 1) * piece, :].astype(F32)


def hidden_kernel(
    lay, sel_ref, p_ref, turned_ref, acc_ref, rim_ref, lo_ref, hi_ref, h_ref, route_ref, full_ref, w_ref, dz_ref
):
    local = p_ref.shape[0]
    h_ref[local:, :] = rim_ref[...]
    peers = len(lay.peers)
    piece = (acc_ref.shape[0] - local) // peers
    assemble(lay, w_ref, (lo_ref, hi_ref), 0)
    for n in strips(w_ref.shape[1]):
        z = dot(p_ref[...], w_ref[:, n])
        s = 1.0 / (1.0 + jnp.exp(-z))
        h_ref[:local, n] = (z * s).astype(BF16)
        dz_ref[:, n] = (acc_ref[:local, n] * s * (1.0 + z * (1.0 - s))).astype(BF16)
        full_ref[:, n] = dot(turned_ref[...], dz_ref[:, n])
    for r in range(peers):
        q = lay.peer(r)
        at = 2 * r * piece
        route_ref[at : at + piece, :] = h_ref[rows(sel_ref[q], piece), :]
        back = acc_ref[pl.ds(pl.multiple_of(local + q * piece, piece), piece), :]
        route_ref[at + piece : at + 2 * piece, :] = back.astype(BF16)


def second_kernel(lay, src_ref, table_ref, tile_ref, og_ref, first_ref, p_ref, keep_ref, send_ref, full_ref):
    blocks, edge = tile_ref.shape[0], tile_ref.shape[2]
    for i in range(blocks):
        p_ref[i * edge : (i + 1) * edge, :] = aggregate_block(i, src_ref, tile_ref, table_ref)
    for n in strips(full_ref.shape[1]):
        full_ref[:, n] = dot(p_ref[...], og_ref[:, n], 0, 0)
    scatter_grad(lay, first_ref, (keep_ref, send_ref), 0)
    scatter_grad(lay, full_ref, (keep_ref, send_ref), 1)


def out_kernel(lay, p_ref, lo_ref, hi_ref, out_ref, w_ref):
    assemble(lay, w_ref, (lo_ref, hi_ref), 1)
    for n in strips(w_ref.shape[1]):
        out_ref[:, n] = dot(p_ref[...], w_ref[:, n]).astype(BF16)


def adam_step(total_nodes, layer, parts, master_ref, first_ref, second_ref):
    shard_rows = master_ref.shape[1]
    at = slice(layer * shard_rows, (layer + 1) * shard_rows)
    shard = parts[0][at, :].astype(F32)
    for p in parts[1:]:
        shard = shard + p[at, :].astype(F32)
    shard = shard / total_nodes
    moment_new = decay_first * first_ref[layer] + (1.0 - decay_first) * shard
    second_new = decay_second * second_ref[layer] + (1.0 - decay_second) * shard * shard
    update = (
        moment_new
        / (1.0 - decay_first**STEP)
        / (jnp.sqrt(second_new / (1.0 - decay_second**STEP)) + epsilon)
    )
    return at, master_ref[layer] - learn_rate * update


def adam_kernel(total_nodes, *refs):
    for layer in range(LAYERS):
        at, after = adam_step(total_nodes, layer, refs[:-4], *refs[-4:-1])
        refs[-1][at, :] = after.astype(BF16)


def settle_kernel(total_nodes, *refs):
    for layer in range(LAYERS):
        refs[-1][layer] = adam_step(total_nodes, layer, refs[:-4], *refs[-4:-1])[1]


def place_rows(lay, half_at, part_ref, out_ref):
    half = lay.count // 2
    size = out_ref.shape[1] // lay.count
    for r in range(half):
        for layer in range(LAYERS):
            src = part_ref.at[pl.ds((r * LAYERS + layer) * size, size), :]
            yield src, out_ref.at[layer, rows(lay.block(half_at * half + r), size), :]


def place_fresh(lay, fresh_ref, feat_ref, grad_ref):
    piece = feat_ref.shape[0] // len(lay.peers)
    for r in range(len(lay.peers)):
        at = rows(lay.peer(r), piece)
        yield fresh_ref.at[pl.ds(2 * r * piece, piece), :], feat_ref.at[at, :]
        yield fresh_ref.at[pl.ds((2 * r + 1) * piece, piece), :], grad_ref.at[at, :]


def run_copies(pairs, sems):
    copies = [pltpu.make_async_copy(src, dst, sems.at[n]) for n, (src, dst) in enumerate(pairs)]
    for c in copies:
        c.start()
    for c in copies:
        c.wait()


def place_kernel(lay, part_ref, fresh_ref, out_ref, feat_ref, grad_ref, sems):
    pairs = [*place_rows(lay, 0, part_ref, out_ref), *place_fresh(lay, fresh_ref, feat_ref, grad_ref)]
    run_copies(pairs, sems)


def finish_kernel(lay, part_ref, held_ref, out_ref, sems):
    run_copies(place_rows(lay, 1, part_ref, out_ref), sems)


def call(body, out_shape, specs, out_specs, scratch, flops, moved, aliases=None):
    return pl.pallas_call(
        body,
        out_shape=out_shape,
        in_specs=specs,
        out_specs=out_specs,
        scratch_shapes=scratch,
        input_output_aliases=aliases or {},
        cost_estimate=pl.CostEstimate(flops=flops, bytes_accessed=moved, transcendentals=0),
        compiler_params=pltpu.CompilerParams(vmem_limit_bytes=40 * 1024 * 1024),
    )


def epoch(
    features,
    tile_src,
    tile_val,
    send_sel,
    stale_features,
    stale_grads,
    out_grad,
    master,
    moment_first,
    moment_second,
):
    peers = lax.axis_size("dom")
    groups = lax.axis_size("grp")
    devices = peers * groups
    local, width = features.shape
    total_nodes = local * devices
    blocks, tiles, edge = tile_val.shape[:3]
    rim = stale_features.shape[0]
    layers, shard_rows = master.shape[:2]
    full_rows = shard_rows * devices
    slots = blocks + rim // edge
    selects = send_sel[0]
    lay = Layout(peers, groups, shard_rows)
    count, size = lay.count, full_rows // lay.count
    half = layers * full_rows // 2
    sds = jax.ShapeDtypeStruct

    def spread_out(lo, hi):
        if lay.packed:
            return lo, hi
        owner = jnp.stack([lay.owner(r) for r in range(devices)])
        inverse = jnp.argmax(owner[None, :] == jnp.arange(devices, dtype=jnp.int32)[:, None], axis=1)
        whole = jnp.concatenate((lo, hi), 0).reshape(devices, layers, shard_rows, width)
        whole = jnp.take(whole, inverse, axis=0).transpose(1, 0, 2, 3).reshape(layers, count, size, width)
        whole = whole.transpose(1, 0, 2, 3).reshape(layers * full_rows, width)
        return whole[:half], whole[half:]

    def draw_in(keep, send):
        if lay.packed:
            return keep, send
        owner = jnp.stack([lay.owner(r) for r in range(devices)])
        whole = jnp.concatenate((keep, send), 0).reshape(count, layers, size, width).transpose(1, 0, 2, 3)
        whole = whole.reshape(layers, devices, shard_rows, width).transpose(1, 0, 2, 3)
        whole = jnp.take(whole, owner, axis=0).reshape(layers * full_rows, width)
        return whole[:half], whole[half:]

    tile_flops = 2 * blocks * tiles * edge * edge * width
    dense_flops = 2 * local * width * width
    tile_bytes = tile_val.size * 2
    node_bytes = features.size * 2
    nodes = sds((local, width), BF16)
    square = sds((full_rows, width), F32)
    grads_half = sds((half, width), BF16)
    listed = (blocks * tiles + slots * (GROUP - 1)) // GROUP
    part = functools.partial

    own, picked = call(
        part(begin_kernel, lay),
        (sds(master.shape, BF16), sds((rim, width), BF16)),
        [HBM, HBM, HBM],
        (VMEM, VMEM),
        [
            pltpu.SMEM((1, peers), jnp.int32),
            pltpu.VMEM(master.shape, F32),
            pltpu.SemaphoreType.DMA((peers + 2,)),
        ],
        0,
        rim * width * 4,
    )(*(pltpu.with_memory_space_constraint(x, pltpu.HBM) for x in (send_sel, master, features)))
    lo, hi, raw_rim = gather_relative(
        own.reshape(layers * shard_rows, width), lay.stages, jnp.split(picked, peers, 0), lay.ways
    )
    lo, hi = spread_out(lo, hi)
    raw_rim = jnp.concatenate(raw_rim, 0)
    turned_tiles, order, goal, _ = call(
        prepare_kernel,
        (
            sds((blocks * tiles + 1, edge, edge), BF16),
            sds((listed * GROUP,), jnp.int32),
            sds((listed,), jnp.int32),
            sds((2,), jnp.int32),
        ),
        [SMEM, HBM],
        (VMEM, SMEM, SMEM, SMEM),
        [
            pltpu.VMEM(tile_val.shape, BF16),
            pltpu.SMEM((slots,), jnp.int32),
            pltpu.SemaphoreType.DMA((blocks,)),
        ],
        0,
        2 * tile_bytes,
    )(tile_src, pltpu.with_memory_space_constraint(tile_val, pltpu.HBM))
    p_first, p_turned = call(
        part(first_kernel, lay),
        (nodes, sds((width, local), BF16)),
        [SMEM, VMEM, VMEM, VMEM],
        (VMEM, VMEM),
        [pltpu.VMEM((local + rim, width), BF16)],
        tile_flops,
        tile_bytes + 2 * node_bytes,
    )(tile_src, features, raw_rim, tile_val)
    acc = call(
        part(spread_kernel, lay),
        sds((local + rim, width), F32),
        [SMEM, SMEM, SMEM, VMEM, VMEM, VMEM, VMEM, VMEM],
        VMEM,
        [pltpu.VMEM((full_rows, width), BF16), pltpu.VMEM((local, width), BF16)],
        tile_flops + dense_flops,
        tile_bytes + 3 * node_bytes,
    )(order, goal, selects, out_grad, turned_tiles, lo, hi, stale_grads)
    sources, route, g_first = call(
        part(hidden_kernel, lay),
        (sds((local + rim, width), BF16), sds((2 * rim, width), BF16), square),
        [SMEM, VMEM, VMEM, VMEM, VMEM, VMEM, VMEM],
        (VMEM, VMEM, VMEM),
        [pltpu.VMEM((full_rows, width), BF16), pltpu.VMEM((local, width), BF16)],
        2 * dense_flops,
        4 * node_bytes,
    )(selects, p_first, p_turned, acc, stale_features, lo, hi)
    p_second, keep, send = call(
        part(second_kernel, lay),
        (nodes, grads_half, grads_half),
        [SMEM, VMEM, VMEM, VMEM, VMEM],
        (VMEM, VMEM, VMEM),
        [pltpu.VMEM((full_rows, width), F32)],
        tile_flops + dense_flops,
        tile_bytes + 3 * node_bytes,
    )(tile_src, sources, tile_val, out_grad, g_first)
    total = reduce_relative(*draw_in(keep, send), lay.stages)
    layer_out = call(
        part(out_kernel, lay),
        nodes,
        [VMEM, VMEM, VMEM],
        VMEM,
        [pltpu.VMEM((full_rows, width), BF16)],
        dense_flops,
        2 * node_bytes,
    )(p_second, lo, hi)
    fresh = jnp.concatenate(exchange(jnp.split(route, peers, 0), lay.ways, range(len(lay.ways))[::-1]), 0)

    state = (*total, master, moment_first, moment_second)
    moved = call(
        part(adam_kernel, total_nodes),
        sds((layers * shard_rows, width), BF16),
        [VMEM] * len(state),
        VMEM,
        [],
        0,
        12 * master.size,
    )(*state)
    master_next = call(
        part(settle_kernel, total_nodes), sds(master.shape, F32), [VMEM] * len(state), VMEM, [], 0, 12 * master.size
    )(*state)
    lo_next, hi_next, _ = gather_relative(moved, lay.stages)
    lo_next, hi_next = spread_out(lo_next, hi_next)
    weights = sds((layers, full_rows, width), BF16)
    weights_next, fresh_features, fresh_grads = call(
        part(place_kernel, lay),
        (weights, sds((rim, width), BF16), sds((rim, width), BF16)),
        [VMEM, VMEM],
        (HBM, HBM, HBM),
        [pltpu.SemaphoreType.DMA((layers * count // 2 + 2 * peers,))],
        0,
        2 * layers * full_rows * width,
    )(lo_next, fresh)
    weights_next = call(
        part(finish_kernel, lay),
        weights,
        [VMEM, HBM],
        HBM,
        [pltpu.SemaphoreType.DMA((layers * count // 2,))],
        0,
        2 * layers * full_rows * width,
        aliases={1: 0},
    )(hi_next, weights_next)
    return (layer_out, fresh_features, fresh_grads, master_next, weights_next)


def solution(mesh):
    placed = (
        P(("dom", "grp"), None),
        P(("dom", "grp"), None),
        P(("dom", "grp"), None, None, None),
        P(("dom", "grp"), None),
        P(("dom", "grp"), None),
        P(("dom", "grp"), None),
        P(("dom", "grp"), None),
        P(None, ("dom", "grp"), None),
        P(None, ("dom", "grp"), None),
        P(None, ("dom", "grp"), None),
    )
    return jax.shard_map(
        epoch,
        mesh=mesh,
        in_specs=placed,
        out_specs=(
            P(("dom", "grp"), None),
            P(("dom", "grp"), None),
            P(("dom", "grp"), None),
            P(None, ("dom", "grp"), None),
            P(),
        ),
        check_vma=False,
    )
```

```python
import functools

import jax
import jax.numpy as jnp
import numpy as np
from jax import lax
from jax.experimental import pallas as pl
from jax.experimental.pallas import tpu as pltpu
from jax.sharding import PartitionSpec as P


STEP = 10


decay_first = 0.9
decay_second = 0.95
learn_rate = 0.01
epsilon = 1e-08

F32 = jnp.float32
BF16 = jnp.bfloat16
AXES = ("dom", "grp")
VMEM = pl.BlockSpec(memory_space=pltpu.VMEM)
SMEM = pl.BlockSpec(memory_space=pltpu.SMEM)
ANY = pl.BlockSpec(memory_space=pl.ANY)
HBM = pl.BlockSpec(memory_space=pltpu.HBM)
PACK = 16
LAYERS = 2
GROUP = 4
STRIP = 256


def plan_stages(nd, ng):
    dom_bits = [1 << i for i in range(nd.bit_length() - 1)]
    grp_bits = [1 << i for i in range(ng.bit_length() - 1)]
    groups = [[(0, b) for b in grp_bits[:1]], [(a, 0) for a in dom_bits[:1]] + [(0, b) for b in grp_bits[1:2]]]
    rest = [(a, 0) for a in dom_bits[1:]] + [(0, b) for b in grp_bits[2:]]
    groups += [rest[i : i + 2] for i in range(0, len(rest), 2)]
    stages = []
    for bits in groups:
        members = [(0, 0)]
        for a, b in bits:
            members = members + [(a ^ x, b ^ y) for x, y in members]
        if len(members) > 1:
            stages.append(members)
    return stages


def cross_stages(stages):
    if len(stages) < 3 or len(stages[1]) != len(stages[2]):
        return stages
    pairs = (stages[1], stages[2]), (stages[2], stages[1])
    return [stages[0]] + [[m + n for m, n in zip(*p)] for p in pairs] + stages[3:]


def relative_order(stages):
    order = [(0, 0, 0, 0)]
    for members in stages:
        wide = [m if len(m) == 4 else m + m for m in members]
        order = [tuple(x ^ y for x, y in zip(at, m[2:] + m[:2] if at[1] % 2 else m)) for at in order for m in wide]
    return order


def swap(x, mask):
    nd, ng = lax.axis_size("dom"), lax.axis_size("grp")
    pairs = []
    for k in range(nd * ng):
        a, b = mask[-2:] if k % 2 else mask[:2]
        pairs.append((k, ((k // ng) ^ a) * ng + ((k % ng) ^ b)))
    return lax.ppermute(x, AXES, pairs)


def gather_relative(shard, stages, parts=(), ways=()):
    places = list(np.ndindex(*[len(members) for members in ways]))
    pieces = dict(zip(places, parts))
    held = shard
    for members in stages[:0:-1]:
        size = held.shape[0]
        got = [held]
        for m in members[1:]:
            lanes = [at for at in pieces for w, way in enumerate(ways) if m in way and at[w] == way.index(m)]
            came = swap(jnp.concatenate([held] + [pieces[at] for at in lanes], 0), m)
            got.append(came[:size])
            if lanes:
                pieces.update(zip(lanes, jnp.split(came[size:], len(lanes), 0)))
        held = jnp.concatenate(got, 0)
    other = swap(held, stages[0][1])
    return held, other, [pieces[at] for at in pieces]


def reduce_relative(keep, send, stages):
    pieces = []
    for k, s in zip(*(jnp.split(x, len(stages[1]), 0) for x in (keep, send))):
        pieces.append((k.astype(F32) + swap(s, stages[0][1]).astype(F32)).astype(BF16))
    for n, members in enumerate(stages[1:]):
        if n:
            pieces = jnp.split(sum(t.astype(F32) for t in terms).astype(BF16), len(members), 0)
        terms = [pieces[0]] + [swap(p, m) for p, m in zip(pieces[1:], members[1:])]
    return terms


def dom_stages(stages):
    split = [[m for m in members if m[1] == 0] for members in stages]
    return [members for members in split if len(members) > 1]


def exchange(parts, ways, turn):
    places = list(np.ndindex(*[len(members) for members in ways]))
    held = dict(zip(places, parts))
    for s in turn:
        for i in range(1, len(ways[s])):
            lanes = [at for at in places if at[s] == i]
            got = swap(jnp.concatenate([held[at] for at in lanes], 0), ways[s][i])
            held.update(zip(lanes, jnp.split(got, len(lanes), 0)))
    return [held[at] for at in places]


class Layout:
    def __init__(self, nd, ng, shard_rows, crossed=False):
        self.stages = plan_stages(nd, ng)
        self.ways = dom_stages(self.stages)
        if crossed:
            self.stages = cross_stages(self.stages)
        self.blocks = relative_order(self.stages)
        self.peers = [m[0] for m in relative_order(self.ways)]
        self.ng = ng
        self.packed = shard_rows % PACK == 0
        self.count = nd * ng if self.packed else nd * ng * shard_rows // PACK

    def owner(self, r):
        a, b, c, d = self.blocks[r]
        group = lax.axis_index("grp")
        if (a, b) != (c, d):
            odd = group % 2
            a, b = a + odd * (c - a), b + odd * (d - b)
        return (lax.axis_index("dom") ^ a) * self.ng + (group ^ b)

    def block(self, r):
        return self.owner(r) if self.packed else r

    def peer(self, r):
        return lax.axis_index("dom") ^ self.peers[r]


def dot(a, b, ca=1, cb=0):
    return lax.dot_general(a, b, (((ca,), (cb,)), ((), ())), preferred_element_type=F32)


def rows(start, size):
    return pl.ds(pl.multiple_of(start * size, size), size)


def strips(width):
    return [slice(n, n + STRIP) for n in range(0, width, STRIP)]


def begin_kernel(lay, sel_hbm, master_hbm, rows_ref, own_ref, out_ref, sel_ref, master_ref, sems):
    peers = len(lay.peers)
    piece = out_ref.shape[0] // peers
    sel_copy = pltpu.make_async_copy(sel_hbm, sel_ref, sems.at[peers])
    master_copy = pltpu.make_async_copy(master_hbm, master_ref, sems.at[peers + 1])
    sel_copy.start()
    master_copy.start()
    sel_copy.wait()
    copies = []
    for r in range(peers):
        src = rows_ref.at[rows(sel_ref[0, lay.peer(r)], piece), :]
        copies.append(pltpu.make_async_copy(src, out_ref.at[pl.ds(r * piece, piece), :], sems.at[r]))
    for c in copies:
        c.start()
    master_copy.wait()
    own_ref[...] = master_ref[...].astype(BF16)
    for c in copies:
        c.wait()


def prepare_kernel(src_ref, tile_hbm, turned_ref, list_ref, goal_ref, bound_ref, tile_ref, count_ref, sems):
    blocks, tiles = tile_ref.shape[:2]
    copies = [pltpu.make_async_copy(tile_hbm.at[i], tile_ref.at[i], sems.at[i]) for i in range(blocks)]
    for c in copies:
        c.start()
    total = blocks * tiles
    slots = count_ref.shape[0]
    groups = goal_ref.shape[0]

    turned_ref[total] = jnp.zeros_like(turned_ref[total])
    for b in range(slots):
        count_ref[b] = 0

    def clear(k, carry):
        list_ref[k] = total
        return carry

    lax.fori_loop(0, groups * GROUP, clear, 0)

    def tally(i, carry):
        for t in range(tiles):
            b = src_ref[i, t]
            count_ref[b] = count_ref[b] + 1
        return carry

    lax.fori_loop(0, blocks, tally, 0)
    first = jnp.int32(0)
    for b in range(slots):
        need = (count_ref[b] + (GROUP - 1)) // GROUP

        def mark(g, carry, b=b):
            goal_ref[g] = b
            return carry

        lax.fori_loop(first, first + need, mark, 0)
        count_ref[b] = first * GROUP
        if b == blocks:
            bound_ref[0] = first * GROUP
        first = first + need

    def rest(g, carry):
        goal_ref[g] = 0
        return carry

    lax.fori_loop(first, groups, rest, 0)
    bound_ref[1] = first * GROUP

    def enter(i, carry):
        for t in range(tiles):
            b = src_ref[i, t]
            at = count_ref[b]
            list_ref[at] = i * tiles + t
            count_ref[b] = at + 1
        return carry

    lax.fori_loop(0, blocks, enter, 0)
    for i in range(blocks):
        copies[i].wait()
        for t in range(tiles):
            turned_ref[i * tiles + t] = tile_ref[i, t].T


def aggregate_block(i, src_ref, tile_ref, table_ref):
    tiles, edge = tile_ref.shape[1], tile_ref.shape[2]
    left = jnp.concatenate([tile_ref[i, t] for t in range(tiles)], 1)
    right = jnp.concatenate([table_ref[rows(src_ref[i, t], edge), :] for t in range(tiles)], 0)
    return dot(left, right).astype(BF16)


def first_kernel(lay, src_ref, feat_ref, rim_ref, tile_ref, out_ref, turned_ref, table_ref):
    blocks, edge = tile_ref.shape[0], tile_ref.shape[2]
    local = feat_ref.shape[0]
    peers = len(lay.peers)
    piece = rim_ref.shape[0] // peers
    table_ref[:local, :] = feat_ref[...]
    for r in range(peers):
        at = pl.multiple_of(local + lay.peer(r) * piece, piece)
        table_ref[pl.ds(at, piece), :] = rim_ref[r * piece : (r + 1) * piece, :]
    for i in range(blocks):
        out = aggregate_block(i, src_ref, tile_ref, table_ref)
        out_ref[i * edge : (i + 1) * edge, :] = out
        turned_ref[:, i * edge : (i + 1) * edge] = out.T


def assemble(lay, dst_ref, parts, layer):
    size = dst_ref.shape[0] // lay.count
    half = lay.count // len(parts)
    for r in range(lay.count):
        at = ((r % half) * LAYERS + layer) * size
        dst_ref[rows(lay.block(r), size), :] = parts[r // half][at : at + size, :]


def scatter_grad(lay, full_ref, outs, layer):
    size = full_ref.shape[0] // lay.count
    half = lay.count // len(outs)
    for r in range(lay.count):
        at = ((r % half) * LAYERS + layer) * size
        outs[r // half][at : at + size, :] = full_ref[rows(lay.block(r), size), :].astype(BF16)


def spread_kernel(lay, list_ref, goal_ref, sel_ref, og_ref, turned_ref, lo_ref, hi_ref, stale_ref, acc_ref, w_ref, up_ref):
    edge = turned_ref.shape[1]
    blocks = og_ref.shape[0] // edge
    tiles = (turned_ref.shape[0] - 1) // blocks
    peers = len(lay.peers)
    piece = stale_ref.shape[0] // peers
    assemble(lay, w_ref, (lo_ref, hi_ref), 1)
    acc_ref[...] = jnp.zeros_like(acc_ref)
    for n in strips(w_ref.shape[0]):
        up_ref[:, n] = dot(og_ref[...], w_ref[n, :], 1, 1).astype(BF16)

    for g in range(goal_ref.shape[0]):
        ks = [list_ref[g * GROUP + j] for j in range(GROUP)]
        left = jnp.concatenate([turned_ref[k] for k in ks], 1)
        right = jnp.concatenate([up_ref[rows(jnp.minimum(k // tiles, blocks - 1), edge), :] for k in ks], 0)
        acc_ref[rows(goal_ref[g], edge), :] += dot(left, right)
    for p in range(peers):
        at = rows(sel_ref[p], piece)
        acc_ref[at, :] += stale_ref[p * piece : (p + 1) * piece, :].astype(F32)


def hidden_kernel(
    lay, sel_ref, p_ref, turned_ref, acc_ref, rim_ref, lo_ref, hi_ref, h_ref, route_ref, full_ref, w_ref, dz_ref
):
    local = p_ref.shape[0]
    h_ref[local:, :] = rim_ref[...]
    peers = len(lay.peers)
    piece = (acc_ref.shape[0] - local) // peers
    assemble(lay, w_ref, (lo_ref, hi_ref), 0)
    for n in strips(w_ref.shape[1]):
        z = dot(p_ref[...], w_ref[:, n])
        s = 1.0 / (1.0 + jnp.exp(-z))
        h_ref[:local, n] = (z * s).astype(BF16)
        dz_ref[:, n] = (acc_ref[:local, n] * s * (1.0 + z * (1.0 - s))).astype(BF16)
        full_ref[:, n] = dot(turned_ref[...], dz_ref[:, n])
    for r in range(peers):
        q = lay.peer(r)
        at = 2 * r * piece
        route_ref[at : at + piece, :] = h_ref[rows(sel_ref[q], piece), :]
        back = acc_ref[pl.ds(pl.multiple_of(local + q * piece, piece), piece), :]
        route_ref[at + piece : at + 2 * piece, :] = back.astype(BF16)


def second_kernel(lay, src_ref, table_ref, tile_ref, og_ref, first_ref, p_ref, keep_ref, send_ref, full_ref):
    blocks, edge = tile_ref.shape[0], tile_ref.shape[2]
    for i in range(blocks):
        p_ref[i * edge : (i + 1) * edge, :] = aggregate_block(i, src_ref, tile_ref, table_ref)
    for n in strips(full_ref.shape[1]):
        full_ref[:, n] = dot(p_ref[...], og_ref[:, n], 0, 0)
    scatter_grad(lay, first_ref, (keep_ref, send_ref), 0)
    scatter_grad(lay, full_ref, (keep_ref, send_ref), 1)


def out_kernel(lay, p_ref, lo_ref, hi_ref, out_ref, w_ref):
    assemble(lay, w_ref, (lo_ref, hi_ref), 1)
    for n in strips(w_ref.shape[1]):
        out_ref[:, n] = dot(p_ref[...], w_ref[:, n]).astype(BF16)


def adam_step(total_nodes, layer, parts, master_ref, first_ref, second_ref):
    shard_rows = master_ref.shape[1]
    at = slice(layer * shard_rows, (layer + 1) * shard_rows)
    shard = parts[0][at, :].astype(F32)
    for p in parts[1:]:
        shard = shard + p[at, :].astype(F32)
    shard = shard / total_nodes
    moment_new = decay_first * first_ref[layer] + (1.0 - decay_first) * shard
    second_new = decay_second * second_ref[layer] + (1.0 - decay_second) * shard * shard
    update = (
        moment_new
        / (1.0 - decay_first**STEP)
        / (jnp.sqrt(second_new / (1.0 - decay_second**STEP)) + epsilon)
    )
    return at, master_ref[layer] - learn_rate * update


def adam_kernel(total_nodes, *refs):
    for layer in range(LAYERS):
        at, after = adam_step(total_nodes, layer, refs[:-4], *refs[-4:-1])
        refs[-1][at, :] = after.astype(BF16)


def settle_kernel(total_nodes, *refs):
    for layer in range(LAYERS):
        refs[-1][layer] = adam_step(total_nodes, layer, refs[:-4], *refs[-4:-1])[1]


def place_rows(lay, half_at, part_ref, out_ref):
    half = lay.count // 2
    size = out_ref.shape[1] // lay.count
    for r in range(half):
        for layer in range(LAYERS):
            src = part_ref.at[pl.ds((r * LAYERS + layer) * size, size), :]
            yield src, out_ref.at[layer, rows(lay.block(half_at * half + r), size), :]


def place_fresh(lay, fresh_ref, feat_ref, grad_ref):
    piece = feat_ref.shape[0] // len(lay.peers)
    for r in range(len(lay.peers)):
        at = rows(lay.peer(r), piece)
        yield fresh_ref.at[pl.ds(2 * r * piece, piece), :], feat_ref.at[at, :]
        yield fresh_ref.at[pl.ds((2 * r + 1) * piece, piece), :], grad_ref.at[at, :]


def run_copies(pairs, sems):
    copies = [pltpu.make_async_copy(src, dst, sems.at[n]) for n, (src, dst) in enumerate(pairs)]
    for c in copies:
        c.start()
    for c in copies:
        c.wait()


def place_kernel(lay, part_ref, fresh_ref, out_ref, feat_ref, grad_ref, sems):
    pairs = [*place_rows(lay, 0, part_ref, out_ref), *place_fresh(lay, fresh_ref, feat_ref, grad_ref)]
    run_copies(pairs, sems)


def finish_kernel(lay, part_ref, held_ref, out_ref, sems):
    run_copies(place_rows(lay, 1, part_ref, out_ref), sems)


def call(body, out_shape, specs, out_specs, scratch, flops, moved, aliases=None):
    return pl.pallas_call(
        body,
        out_shape=out_shape,
        in_specs=specs,
        out_specs=out_specs,
        scratch_shapes=scratch,
        input_output_aliases=aliases or {},
        cost_estimate=pl.CostEstimate(flops=flops, bytes_accessed=moved, transcendentals=0),
        compiler_params=pltpu.CompilerParams(vmem_limit_bytes=40 * 1024 * 1024),
    )


def epoch(
    features,
    tile_src,
    tile_val,
    send_sel,
    stale_features,
    stale_grads,
    out_grad,
    master,
    moment_first,
    moment_second,
):
    peers = lax.axis_size("dom")
    groups = lax.axis_size("grp")
    devices = peers * groups
    local, width = features.shape
    total_nodes = local * devices
    blocks, tiles, edge = tile_val.shape[:3]
    rim = stale_features.shape[0]
    layers, shard_rows = master.shape[:2]
    full_rows = shard_rows * devices
    slots = blocks + rim // edge
    selects = send_sel[0]
    lay = Layout(peers, groups, shard_rows)
    turned = Layout(peers, groups, shard_rows, True)
    count, size = lay.count, full_rows // lay.count
    half = layers * full_rows // 2
    sds = jax.ShapeDtypeStruct

    def spread_out(lay, lo, hi):
        if lay.packed:
            return lo, hi
        owner = jnp.stack([lay.owner(r) for r in range(devices)])
        inverse = jnp.argmax(owner[None, :] == jnp.arange(devices, dtype=jnp.int32)[:, None], axis=1)
        whole = jnp.concatenate((lo, hi), 0).reshape(devices, layers, shard_rows, width)
        whole = jnp.take(whole, inverse, axis=0).transpose(1, 0, 2, 3).reshape(layers, count, size, width)
        whole = whole.transpose(1, 0, 2, 3).reshape(layers * full_rows, width)
        return whole[:half], whole[half:]

    def draw_in(lay, keep, send):
        if lay.packed:
            return keep, send
        owner = jnp.stack([lay.owner(r) for r in range(devices)])
        whole = jnp.concatenate((keep, send), 0).reshape(count, layers, size, width).transpose(1, 0, 2, 3)
        whole = whole.reshape(layers, devices, shard_rows, width).transpose(1, 0, 2, 3)
        whole = jnp.take(whole, owner, axis=0).reshape(layers * full_rows, width)
        return whole[:half], whole[half:]

    tile_flops = 2 * blocks * tiles * edge * edge * width
    dense_flops = 2 * local * width * width
    tile_bytes = tile_val.size * 2
    node_bytes = features.size * 2
    nodes = sds((local, width), BF16)
    square = sds((full_rows, width), F32)
    grads_half = sds((half, width), BF16)
    listed = (blocks * tiles + slots * (GROUP - 1)) // GROUP
    part = functools.partial

    own, picked = call(
        part(begin_kernel, lay),
        (sds(master.shape, BF16), sds((rim, width), BF16)),
        [HBM, HBM, HBM],
        (VMEM, VMEM),
        [
            pltpu.SMEM((1, peers), jnp.int32),
            pltpu.VMEM(master.shape, F32),
            pltpu.SemaphoreType.DMA((peers + 2,)),
        ],
        0,
        rim * width * 4,
    )(*(pltpu.with_memory_space_constraint(x, pltpu.HBM) for x in (send_sel, master, features)))
    lo, hi, raw_rim = gather_relative(
        own.reshape(layers * shard_rows, width), lay.stages, jnp.split(picked, peers, 0), lay.ways
    )
    lo, hi = spread_out(lay, lo, hi)
    raw_rim = jnp.concatenate(raw_rim, 0)
    turned_tiles, order, goal, _ = call(
        prepare_kernel,
        (
            sds((blocks * tiles + 1, edge, edge), BF16),
            sds((listed * GROUP,), jnp.int32),
            sds((listed,), jnp.int32),
            sds((2,), jnp.int32),
        ),
        [SMEM, HBM],
        (VMEM, SMEM, SMEM, SMEM),
        [
            pltpu.VMEM(tile_val.shape, BF16),
            pltpu.SMEM((slots,), jnp.int32),
            pltpu.SemaphoreType.DMA((blocks,)),
        ],
        0,
        2 * tile_bytes,
    )(tile_src, pltpu.with_memory_space_constraint(tile_val, pltpu.HBM))
    p_first, p_turned = call(
        part(first_kernel, lay),
        (nodes, sds((width, local), BF16)),
        [SMEM, VMEM, VMEM, VMEM],
        (VMEM, VMEM),
        [pltpu.VMEM((local + rim, width), BF16)],
        tile_flops,
        tile_bytes + 2 * node_bytes,
    )(tile_src, features, raw_rim, tile_val)
    acc = call(
        part(spread_kernel, lay),
        sds((local + rim, width), F32),
        [SMEM, SMEM, SMEM, VMEM, VMEM, VMEM, VMEM, VMEM],
        VMEM,
        [pltpu.VMEM((full_rows, width), BF16), pltpu.VMEM((local, width), BF16)],
        tile_flops + dense_flops,
        tile_bytes + 3 * node_bytes,
    )(order, goal, selects, out_grad, turned_tiles, lo, hi, stale_grads)
    sources, route, g_first = call(
        part(hidden_kernel, lay),
        (sds((local + rim, width), BF16), sds((2 * rim, width), BF16), square),
        [SMEM, VMEM, VMEM, VMEM, VMEM, VMEM, VMEM],
        (VMEM, VMEM, VMEM),
        [pltpu.VMEM((full_rows, width), BF16), pltpu.VMEM((local, width), BF16)],
        2 * dense_flops,
        4 * node_bytes,
    )(selects, p_first, p_turned, acc, stale_features, lo, hi)
    p_second, keep, send = call(
        part(second_kernel, turned),
        (nodes, grads_half, grads_half),
        [SMEM, VMEM, VMEM, VMEM, VMEM],
        (VMEM, VMEM, VMEM),
        [pltpu.VMEM((full_rows, width), F32)],
        tile_flops + dense_flops,
        tile_bytes + 3 * node_bytes,
    )(tile_src, sources, tile_val, out_grad, g_first)
    total = reduce_relative(*draw_in(turned, keep, send), turned.stages)
    layer_out = call(
        part(out_kernel, lay),
        nodes,
        [VMEM, VMEM, VMEM],
        VMEM,
        [pltpu.VMEM((full_rows, width), BF16)],
        dense_flops,
        2 * node_bytes,
    )(p_second, lo, hi)
    fresh = jnp.concatenate(exchange(jnp.split(route, peers, 0), lay.ways, range(len(lay.ways))[::-1]), 0)

    state = (*total, master, moment_first, moment_second)
    moved = call(
        part(adam_kernel, total_nodes),
        sds((layers * shard_rows, width), BF16),
        [VMEM] * len(state),
        VMEM,
        [],
        0,
        12 * master.size,
    )(*state)
    master_next = call(
        part(settle_kernel, total_nodes), sds(master.shape, F32), [VMEM] * len(state), VMEM, [], 0, 12 * master.size
    )(*state)
    lo_next, hi_next, _ = gather_relative(moved, turned.stages)
    lo_next, hi_next = spread_out(turned, lo_next, hi_next)
    weights = sds((layers, full_rows, width), BF16)
    weights_next, fresh_features, fresh_grads = call(
        part(place_kernel, turned),
        (weights, sds((rim, width), BF16), sds((rim, width), BF16)),
        [VMEM, VMEM],
        (HBM, HBM, HBM),
        [pltpu.SemaphoreType.DMA((layers * count // 2 + 2 * peers,))],
        0,
        2 * layers * full_rows * width,
    )(lo_next, fresh)
    weights_next = call(
        part(finish_kernel, turned),
        weights,
        [VMEM, HBM],
        HBM,
        [pltpu.SemaphoreType.DMA((layers * count // 2,))],
        0,
        2 * layers * full_rows * width,
        aliases={1: 0},
    )(hi_next, weights_next)
    return (layer_out, fresh_features, fresh_grads, master_next, weights_next)


def solution(mesh):
    placed = (
        P(("dom", "grp"), None),
        P(("dom", "grp"), None),
        P(("dom", "grp"), None, None, None),
        P(("dom", "grp"), None),
        P(("dom", "grp"), None),
        P(("dom", "grp"), None),
        P(("dom", "grp"), None),
        P(None, ("dom", "grp"), None),
        P(None, ("dom", "grp"), None),
        P(None, ("dom", "grp"), None),
    )
    return jax.shard_map(
        epoch,
        mesh=mesh,
        in_specs=placed,
        out_specs=(
            P(("dom", "grp"), None),
            P(("dom", "grp"), None),
            P(("dom", "grp"), None),
            P(None, ("dom", "grp"), None),
            P(),
        ),
        check_vma=False,
    )
```
